128 devices in a mesh: band: 8 (over y_hi, z), fft: 16 (over y_lo, x, core).
Axes of the slice: x: 4, y: 4 (y_hi: 2, y_lo: 2; y = y_hi * 2 + y_lo), z: 4, core: 2. Of those that a mesh axis runs over, the one named last changes fastest.
Arguments:
- band_coeffs: float32 [16, 1024, 192], P('band', 'fft'), may hold values from -6 to 6
- potential: float32 [192, 192, 192], P('fft'), may hold values from -12 to 12
- stick_column: int32 [1024], replicated, may hold values from 0 to 9215, as said below
- stick_length: int32 [1024], P('fft'), may hold values from 1 to 96
- orbitals: bfloat16 [512, 1024, 192], P(None, ('band', 'fft')), may hold values from -0.078125 to 0.078125
Outputs:
- applied: bfloat16 [16, 1024, 192], P('band', 'fft')
- margin: float32 [512, 32], P(('band', 'fft'))
The draws below stay inside these ranges and needn't reach their ends.
Inputs may be any that keep to these rules, and one draw needn't show every extreme that they name: `stick_column`: distinct columns of a 96 x 96 frequency box; column q stands for gx = q // 96 - 96/2 and gy = q % 96 - 96/2.
All inputs are finite; a program needn't handle non-finite values.
Results may differ from the reference program's by a relative error of at most 0.0055.
Values may be sent and summed in bfloat16 or wider, within the bound.
A program may use at most 64 MiB of HBM per device.

```python
import jax
import jax.numpy as jnp
from jax import lax

GRID = 192
HALF = 96
STK_DEV = 64
ORBITALS = 512
BANDS = 16
STICKS = 1024
N_BAND = 8
N_FFT = 16


def draw_stick_column(key, part):
    box_cells = HALF * HALF
    inner_set = 1 + jax.random.permutation(jax.random.fold_in(key, 11), box_cells - 2)[:STICKS - 2]
    chosen = jnp.concatenate([inner_set.astype(jnp.int32), jnp.array([0, box_cells - 1], jnp.int32)])
    shuffle_order = jax.random.permutation(jax.random.fold_in(key, 12), STICKS)
    return chosen[shuffle_order].astype(jnp.int32)


def draw_stick_length(key, part):
    values = jax.random.randint(jax.random.fold_in(key, 13), (STICKS,), 1, HALF + 1, dtype=jnp.int32)
    where_most = jax.random.randint(jax.random.fold_in(key, 14), (), 0, STICKS, dtype=jnp.int32)
    return values.at[where_most].set(HALF).astype(jnp.int32)


def spiked(values, rng, source, target, blocks, factor):
    def block_of(position):
        return (jnp.arange(values.shape[position]) // (values.shape[position] // blocks)).reshape((-1,) + (1,) * (values.ndim - 1 - position))

    near = jax.random.permutation(rng, blocks)[block_of(target)]
    second = (block_of(target) + blocks // 2) % blocks
    return jnp.where((block_of(source) == near) | (block_of(source) == second), factor * values, values)


def block_levels(key, shape, pieces, smallest, largest):
    factor_of = 1.0
    for axis_at, shards_of in pieces:
        steps = jax.random.uniform(jax.random.fold_in(jax.random.fold_in(key, 6), axis_at), (shards_of,), jnp.float32, smallest / len(pieces), largest / len(pieces))
        factor_of = factor_of * jnp.repeat(jnp.exp(steps), shape[axis_at] // shards_of).reshape((-1,) + (1,) * (len(shape) - 1 - axis_at))
    return factor_of


def centred(key, shape, deviation, limit, split=(), held_as=jnp.bfloat16):
    values = deviation * jax.random.normal(key, shape, jnp.float32)
    if split:
        values = values * block_levels(key, shape, split, -0.22, 0.18)
    return jnp.clip(values, -limit, limit).astype(held_as)


def noise_with(own_key, dims, width, bound, split, heavy, held_as=jnp.bfloat16):
    entries = width * jax.random.normal(own_key, dims, jnp.float32)
    if split:
        entries = entries * block_levels(own_key, dims, split, -0.22, 0.18)
    return jnp.clip(spiked(entries, jax.random.fold_in(own_key, 3), *heavy), -bound, bound).astype(held_as)


def setup_inputs(seed: int = 0) -> dict:
    streams_of = jax.random.split(jax.random.key(seed), 6)
    band_coeffs = centred(streams_of[0], (BANDS, STICKS, GRID), 1.0, 6.0, ((0, 8), (1, 16)), jnp.float32)
    potential = centred(streams_of[1], (GRID, GRID, GRID), 2.0, 12.0, ((0, 16),), jnp.float32)
    stick_column = draw_stick_column(jax.random.fold_in(streams_of[5], 71), 0)
    stick_length = draw_stick_length(jax.random.fold_in(streams_of[5], 71), 0)
    orbitals = noise_with(streams_of[4], (ORBITALS, STICKS, GRID), (STICKS * HALF) ** -0.5, 0.078125, ((1, 128),), (1, 0, 128, 5.5))
    return {"band_coeffs": band_coeffs, "potential": potential, "stick_column": stick_column, "stick_length": stick_length, "orbitals": orbitals}


def reference(band_coeffs, potential, stick_column, stick_length, orbitals):
    half_mid = HALF // 2
    z_freq = jnp.arange(HALF, dtype=jnp.int32) - half_mid
    stick_len = stick_length[:, None]
    live_slots = (z_freq[None, :] >= -(stick_len // 2)) & (z_freq[None, :] < stick_len - stick_len // 2)
    x_freq = stick_column // HALF - half_mid
    y_freq = stick_column % HALF - half_mid
    kinetic = (x_freq[:, None] ** 2 + y_freq[:, None] ** 2 + z_freq[None, :] ** 2).astype(jnp.float32) * (2.0 / (HALF * HALF))
    z_index = (z_freq % GRID)[None, :]
    x_index = (x_freq % GRID)[:, None]
    y_index = (y_freq % GRID)[:, None]

    def apply_band(coeffs_in):
        real_in = jnp.where(live_slots, coeffs_in[:, :HALF], jnp.float32(0.0))
        imag_in = jnp.where(live_slots, coeffs_in[:, HALF:], jnp.float32(0.0))
        box_real = jnp.zeros((GRID, GRID, GRID), real_in.dtype).at[z_index, x_index, y_index].set(real_in)
        box_imag = jnp.zeros((GRID, GRID, GRID), real_in.dtype).at[z_index, x_index, y_index].set(imag_in)
        real_field = jnp.fft.ifftn(lax.complex(box_real, box_imag)) * potential
        picked = jnp.fft.fftn(real_field)[z_index, x_index, y_index]
        h_real = jnp.where(live_slots, kinetic * real_in + jnp.real(picked), jnp.float32(0.0))
        h_imag = jnp.where(live_slots, kinetic * imag_in + jnp.imag(picked), jnp.float32(0.0))
        return jnp.concatenate([h_real, h_imag], axis=1).astype(jnp.bfloat16)

    applied = lax.map(apply_band, band_coeffs)
    real_part = applied[:, :, :HALF]
    imag_part = applied[:, :, HALF:]
    swapped = jnp.concatenate([imag_part, -real_part], axis=2)
    stacked = jnp.concatenate([applied, swapped], axis=0)
    stacked = stacked.reshape(2 * BANDS, N_FFT, N_BAND, STK_DEV // N_BAND, GRID)
    stacked = stacked.transpose(0, 2, 1, 3, 4).reshape(2 * BANDS, STICKS * GRID)
    orbital_rows = orbitals.reshape(ORBITALS, STICKS * GRID)
    margin = lax.dot_general(orbital_rows, stacked, (((1,), (1,)), ((), ())), preferred_element_type=jnp.float32)
    return applied, margin
```

```python
import functools
import math

import jax
import jax.numpy as jnp
import numpy as np
from jax import lax
from jax.experimental import pallas as pl
from jax.experimental.pallas import tpu as pltpu
from jax.sharding import PartitionSpec as P

BF = jnp.bfloat16
F32 = jnp.float32
MESH = pl.DeviceIdType.MESH
HIGH = lax.Precision.HIGHEST
VM = pl.BlockSpec(memory_space=pltpu.VMEM)


def dft_tables(half, grid):
    pad_to = -(-half // 128) * 128
    freq = np.arange(half) - half // 2
    angle = (freq[:, None] * np.arange(grid)[None, :] % grid) * (2.0 * math.pi / grid)
    co, si = np.cos(angle), np.sin(angle)
    pad = ((0, pad_to - half), (0, 0))
    cp, sp = np.pad(co, pad), np.pad(si, pad)
    fy = np.stack([np.concatenate([cp, -sp], 0), np.concatenate([sp, cp], 0)])
    fx = np.concatenate([np.concatenate([co.T, -si.T], 1), np.concatenate([si.T, co.T], 1)], 0)
    fxb = np.concatenate([np.concatenate([co, si], 1), np.concatenate([-si, co], 1)], 0)
    fyb = np.stack([np.concatenate([cp.T, -sp.T], 1), np.concatenate([sp.T, cp.T], 1)])
    fz = np.stack(
        [np.concatenate([co.T, -si.T], 1), np.concatenate([si.T, co.T], 1)], 1
    ).reshape(2 * grid, 2 * half)
    fzb = np.concatenate(
        [np.stack([co, si], -1).reshape(half, -1), np.stack([-si, co], -1).reshape(half, -1)], 0
    ) / float(grid) ** 3
    return fy, fx, fxb, fyb, fz, fzb


def greet(groups):
    barrier = pltpu.get_barrier_semaphore()
    total = 0
    for axis, n in groups:
        me = lax.axis_index(axis)
        for k in range(1, n):
            pl.semaphore_signal(
                barrier, inc=1, device_id={axis: lax.rem(me + k, n)}, device_id_type=MESH
            )
        total += n - 1
    pl.semaphore_wait(barrier, total)


def exchange(axis, n, src, dst, send_sem, recv_sem):
    me = lax.axis_index(axis)
    copies = []
    for k in range(1, n):
        peer = lax.rem(me + k, n)
        copies.append(
            pltpu.make_async_remote_copy(
                src_ref=src.at[peer],
                dst_ref=dst.at[me],
                send_sem=send_sem.at[k],
                recv_sem=recv_sem.at[k],
                device_id={axis: peer},
                device_id_type=MESH,
            )
        )
        copies[-1].start()
    own = pltpu.make_async_copy(src.at[me], dst.at[me], send_sem.at[0])
    own.start()
    own.wait()
    for copy in copies:
        copy.wait()


def live_of(length, half, lanes_of):
    lane = lax.broadcasted_iota(jnp.int32, lanes_of, 1)
    z_freq = lane % half - half // 2
    return (z_freq >= -(length // 2)) & (z_freq < length - length // 2), z_freq


def columns_kernel(n, coef, length, fz, out, send, send_sem, recv_sem):
    half = coef.shape[1] // 2
    live, _ = live_of(length[...], half, coef.shape)
    masked = jnp.where(live, coef[...], 0.0)
    cols = lax.dot_general(
        fz[...], masked, (((1,), (1,)), ((), ())), precision=HIGH, preferred_element_type=F32
    )
    send[...] = cols.reshape(send.shape).astype(BF)
    greet([("fft", n)])
    exchange("fft", n, send, out, send_sem, recv_sem)


def planes_kernel(half, recv, pot, col, fy, fx, fxb, fyb, out, ox, oxf, wyt, wy, cf, acc):
    nf, rows, lanes = recv.shape
    planes = pot.shape[0]
    sd = lanes // 2
    lane_pad = fy.shape[1] // 2
    for f in range(nf):
        c = col[f : f + 1, :]
        c = jnp.concatenate([c, c], axis=1)
        xs = c // half
        ys = c - xs * half
        sl = slice(f * lanes, (f + 1) * lanes)
        one = (lax.broadcasted_iota(jnp.int32, (half, lanes), 0) == xs).astype(F32)
        oxf[:, sl] = one
        ox[:, sl] = one.astype(BF)
        r = lax.broadcasted_iota(jnp.int32, (2 * lane_pad, lanes), 0)
        b = lax.broadcasted_iota(jnp.int32, (2 * lane_pad, lanes), 1) // sd
        w = (r == ys + b * lane_pad).astype(F32)
        wyt[:, sl] = w.astype(BF)
        wy[sl, :] = w.T.astype(BF)
        cf[f] = recv[f].astype(F32)

    def step(p, carry):
        parts = []
        for c in range(2):
            pieces = []
            for f in range(nf):
                row = cf[f, pl.ds(2 * p + c, 1), :]
                sl = slice(f * lanes, (f + 1) * lanes)
                pieces.append(ox[:, sl] * jnp.broadcast_to(row, (half, lanes)).astype(BF))
            parts.append(jnp.concatenate(pieces, axis=1))
        spread = jnp.concatenate(parts, axis=0)
        g = jnp.dot(spread, wy[...], preferred_element_type=F32).astype(BF)
        first, second = slice(0, lane_pad), slice(lane_pad, 2 * lane_pad)
        gs = jnp.concatenate(
            [jnp.concatenate([g[:half, b], g[half:, b]], axis=1) for b in (first, second)], axis=0
        )
        ar = jnp.dot(gs, fy[0], preferred_element_type=F32).astype(BF)
        ai = jnp.dot(gs, fy[1], preferred_element_type=F32).astype(BF)
        v = pot[p]
        grid = v.shape[0]
        br, bi = [], []
        for b in range(2):
            rows_b = slice(b * half, (b + 1) * half)
            a = jnp.concatenate([ar[rows_b], ai[rows_b]], axis=0)
            psi = jnp.dot(fx[...], a, preferred_element_type=F32)
            w = jnp.concatenate([psi[:grid] * v, psi[grid:] * v], axis=0).astype(BF)
            bk = jnp.dot(fxb[...], w, preferred_element_type=F32).astype(BF)
            br.append(bk[:half])
            bi.append(bk[half:])
        cc = jnp.dot(jnp.concatenate(br, axis=0), fyb[0], preferred_element_type=F32)
        cc = cc + jnp.dot(jnp.concatenate(bi, axis=0), fyb[1], preferred_element_type=F32)
        cc = cc.astype(BF)
        pk = jnp.concatenate(
            [jnp.concatenate([cc[:half, c], cc[half:, c]], axis=1) for c in (first, second)], axis=0
        )
        d = jnp.dot(pk, wyt[...], preferred_element_type=F32)
        for c in range(2):
            s = jnp.sum(d[c * half : (c + 1) * half] * oxf[...], axis=0, keepdims=True)
            for f in range(nf):
                acc[f, pl.ds(2 * p + c, 1), :] = s[:, f * lanes : (f + 1) * lanes]
        return carry

    lax.fori_loop(0, planes, step, 0)
    for f in range(nf):
        out[f] = acc[f].astype(BF)


def sticks_kernel(
    n_fft, n_band, scale, picked, coef, length, square, fzb,
    applied, gathered, recv, send, fft_send, fft_recv, band_send, band_recv,
):
    greet([("fft", n_fft), ("band", n_band)])
    exchange("fft", n_fft, picked, recv, fft_send, fft_recv)
    half = coef.shape[1] // 2
    sticks = coef.shape[0] // 2
    group = sticks // n_band
    values = recv[...].astype(F32).reshape(-1, recv.shape[2])
    local = jnp.dot(fzb[...], values, precision=HIGH, preferred_element_type=F32).T
    live, z_freq = live_of(length[...], half, coef.shape)
    kinetic = (square[...] + z_freq * z_freq).astype(F32) * scale
    h = jnp.where(live, kinetic * coef[...] + local, 0.0)
    applied[...] = h.astype(BF)
    for r in range(n_band):
        one, two = r * group, sticks + r * group
        send[r] = jnp.concatenate([h[one : one + group], h[two : two + group]], axis=0).astype(BF)
    exchange("band", n_band, send, gathered, band_send, band_recv)


def reduce_kernel(n_fft, n_band, part, out, recv, mid, last, fft_send, fft_recv, band_send, band_recv):
    greet([("fft", n_fft), ("band", n_band)])
    exchange("fft", n_fft, part, recv, fft_send, fft_recv)
    total = recv[0]
    for f in range(1, n_fft):
        total = total + recv[f]
    for r in range(n_band):
        mid[r] = total[r : r + 1]
    exchange("band", n_band, mid, last, band_send, band_recv)
    total = last[0]
    for r in range(1, n_band):
        total = total + last[r]
    out[...] = total


def dma(n):
    return pltpu.SemaphoreType.DMA((n,))


def per_device(n_band, n_fft, band_coeffs, potential, stick_column, stick_length, orbitals):
    bands, sticks, width = band_coeffs.shape
    half = width // 2
    grid = potential.shape[1]
    planes = potential.shape[0]
    fy, fx, fxb, fyb, fz, fzb = dft_tables(half, grid)
    coef = band_coeffs.reshape(bands * sticks, width)
    first = lax.axis_index("fft") * sticks
    own = lax.dynamic_slice_in_dim(stick_column, first, sticks)
    x_freq = own // half - half // 2
    y_freq = own % half - half // 2
    square = jnp.tile(x_freq**2 + y_freq**2, bands)[:, None]
    length = jnp.tile(stick_length, bands)[:, None]
    block = (n_fft, 2 * planes, bands * sticks)

    def params(cid):
        return pltpu.CompilerParams(collective_id=cid, has_side_effects=True)

    recv = pl.pallas_call(
        functools.partial(columns_kernel, n_fft),
        out_shape=jax.ShapeDtypeStruct(block, BF),
        in_specs=[VM] * 3,
        out_specs=VM,
        scratch_shapes=[pltpu.VMEM(block, BF), dma(n_fft), dma(n_fft)],
        compiler_params=params(0),
        name="columns",
    )(coef, length, jnp.asarray(fz, F32))

    flat = n_fft * bands * sticks
    picked = pl.pallas_call(
        functools.partial(planes_kernel, half),
        out_shape=jax.ShapeDtypeStruct(block, BF),
        in_specs=[VM] * 7,
        out_specs=VM,
        scratch_shapes=[
            pltpu.VMEM((half, flat), BF),
            pltpu.VMEM((half, flat), F32),
            pltpu.VMEM((fy.shape[1], flat), BF),
            pltpu.VMEM((flat, fy.shape[1]), BF),
            pltpu.VMEM(block, F32),
            pltpu.VMEM(block, F32),
        ],
        compiler_params=pltpu.CompilerParams(vmem_limit_bytes=48 * 1024 * 1024),
        name="planes",
    )(
        recv, potential, stick_column.reshape(n_fft, sticks),
        jnp.asarray(fy, BF), jnp.asarray(fx, BF), jnp.asarray(fxb, BF), jnp.asarray(fyb, BF),
    )

    group = sticks // n_band
    swap = (n_band, bands * group, width)
    applied, gathered = pl.pallas_call(
        functools.partial(sticks_kernel, n_fft, n_band, 2.0 / (half * half)),
        out_shape=(jax.ShapeDtypeStruct(coef.shape, BF), jax.ShapeDtypeStruct(swap, BF)),
        in_specs=[VM] * 5,
        out_specs=(VM, VM),
        scratch_shapes=[
            pltpu.VMEM(block, BF), pltpu.VMEM(swap, BF),
            dma(n_fft), dma(n_fft), dma(n_band), dma(n_band),
        ],
        compiler_params=params(1),
        name="sticks",
    )(picked, coef, length, square, jnp.asarray(fzb, F32))

    gathered = gathered.reshape(n_band * bands, group, width)
    swapped = jnp.concatenate([gathered[:, :, half:], -gathered[:, :, :half]], 2)
    stacked = jnp.concatenate([gathered, swapped], 0).reshape(2 * n_band * bands, -1)
    partial = lax.dot_general(
        orbitals.reshape(orbitals.shape[0], -1), stacked, (((1,), (1,)), ((), ())),
        preferred_element_type=F32,
    )
    owned = orbitals.shape[0] // (n_band * n_fft) * partial.shape[1]
    partial = partial.reshape(n_band, n_fft, owned).transpose(1, 0, 2)
    margin = pl.pallas_call(
        functools.partial(reduce_kernel, n_fft, n_band),
        out_shape=jax.ShapeDtypeStruct((1, owned), F32),
        in_specs=[VM],
        out_specs=VM,
        scratch_shapes=[
            pltpu.VMEM(partial.shape, F32),
            pltpu.VMEM((n_band, 1, owned), F32), pltpu.VMEM((n_band, 1, owned), F32),
            dma(n_fft), dma(n_fft), dma(n_band), dma(n_band),
        ],
        compiler_params=params(2),
        name="reduce",
    )(partial)
    return applied.reshape(band_coeffs.shape), margin.reshape(-1, 2 * n_band * bands)


def solution(mesh):
    placed = (
        P("band", "fft", None),
        P("fft", None, None),
        P(),
        P("fft"),
        P(None, ("band", "fft"), None),
    )
    return jax.shard_map(
        functools.partial(per_device, mesh.shape["band"], mesh.shape["fft"]),
        mesh=mesh,
        in_specs=placed,
        out_specs=(P("band", "fft", None), P(("band", "fft"), None)),
        check_vma=False,
    )
```

```python
import functools
import math

import jax
import jax.numpy as jnp
import numpy as np
from jax import lax
from jax.experimental import pallas as pl
from jax.experimental.pallas import tpu as pltpu
from jax.sharding import PartitionSpec as P

BF = jnp.bfloat16
F32 = jnp.float32
I32 = jnp.int32
MESH = pl.DeviceIdType.MESH
LANES = 128
SUB = 8


def dft_tables(half, grid):
    freq = np.arange(half) - half // 2
    angle = (freq[:, None] * np.arange(grid)[None, :] % grid) * (2.0 * math.pi / grid)
    co, si = np.cos(angle), np.sin(angle)
    cp, sp = (np.concatenate([a, np.zeros((LANES - half, grid))], 0) for a in (co, si))
    near, far = slice(0, LANES), slice(LANES, grid)

    def ahead(part):
        return (np.concatenate([cp[:, part], -sp[:, part]], 0),
                np.concatenate([sp[:, part], cp[:, part]], 0))

    def back(part):
        return (np.concatenate([cp[:, part].T, -sp[:, part].T], 1),
                np.concatenate([sp[:, part].T, cp[:, part].T], 1))

    y_near = np.concatenate(ahead(near), 1)
    r, i = ahead(far)
    o = np.zeros_like(r)
    y_far = np.concatenate([np.concatenate([r, o, i, o], 1), np.concatenate([o, r, o, i], 1)], 0)
    x_ahead = np.concatenate(
        [np.concatenate([co.T, -si.T], 1), np.concatenate([si.T, co.T], 1)], 0)
    x_back = np.concatenate([np.concatenate([co, si], 1), np.concatenate([-si, co], 1)], 0)
    yb_near = np.concatenate(back(near), 0)
    r, i = back(far)
    o = np.zeros_like(r)
    yb_far = np.concatenate([np.concatenate([r, o, i, o], 0), np.concatenate([o, r, o, i], 0)], 1)
    z_ahead = np.stack(
        [np.concatenate([co.T, -si.T], 1), np.concatenate([si.T, co.T], 1)], 1
    ).reshape(2 * grid, 2 * half)
    z_back = np.concatenate(
        [np.stack([co, si], -1).reshape(half, -1), np.stack([-si, co], -1).reshape(half, -1)], 0
    ) / float(grid) ** 3

    def two_part(a):
        high = a.astype(np.float32).astype(BF)
        low = (a - high.astype(np.float64)).astype(np.float32).astype(BF)
        return np.stack([high, low])

    plain = [a.astype(np.float32).astype(BF) for a in (y_near, y_far, x_ahead, x_back, yb_near, yb_far)]
    return [two_part(z_ahead)] + plain + [two_part(z_back)]


def dot(a, b):
    return jnp.dot(a, b, preferred_element_type=F32)


def dot_t(a, b):
    return lax.dot_general(a, b, (((1,), (1,)), ((), ())), preferred_element_type=F32)


def iota(shape, dim):
    return lax.broadcasted_iota(I32, shape, dim)


def join(parts, axis):
    return jnp.concatenate(parts, axis=axis)


class Exchange:
    def __init__(self, axis, n, src, dst, send_sem, recv_sem):
        me = lax.axis_index(axis)
        self.copies = []
        for k in range(1, n):
            peer = lax.rem(me + k, n)
            self.copies.append(pltpu.make_async_remote_copy(
                src_ref=src.at[peer], dst_ref=dst.at[me],
                send_sem=send_sem.at[k], recv_sem=recv_sem.at[k],
                device_id={axis: peer}, device_id_type=MESH))
        self.own = pltpu.make_async_copy(src.at[me], dst.at[me], send_sem.at[0])

    def start(self):
        for copy in self.copies:
            copy.start()
        self.own.start()

    def wait(self):
        self.own.wait()
        for copy in self.copies:
            copy.wait()


def build_cells(half, q, w1, w1t, oxl):
    qq = q[...]
    xs = qq // half
    ys = qq - xs * half
    xh = xs // SUB
    xl = xs - xh * SUB
    cell = xh * LANES + ys
    down = cell.astype(F32).T
    cells, rows = w1t.shape[0], qq.shape[0]
    for k in range(rows):
        sl = slice(LANES * k, LANES * (k + 1))
        w1t[:, sl] = (iota((cells, LANES), 0) == cell[k : k + 1, :]).astype(F32).astype(BF)
        w1[sl, :] = (iota((LANES, cells), 1).astype(F32) == down[:, k : k + 1]).astype(F32).astype(BF)
        oxl[:, sl] = (iota((SUB, LANES), 0) == xl[k : k + 1, :]).astype(F32)


def spread_sticks(recv, oxl, cfb, lhs):
    nf, rows, lanes = recv.shape
    low = iota((rows, lanes), 1) < lanes // 2
    for k in range(nf // 2):
        a = recv[2 * k].astype(F32)
        b = recv[2 * k + 1].astype(F32)
        sl = slice(lanes * k, lanes * (k + 1))
        cfb[0, :, sl] = jnp.where(low, a, pltpu.roll(b, lanes // 2, 1))
        cfb[1, :, sl] = jnp.where(low, pltpu.roll(a, lanes // 2, 1), b)
    count = cfb.shape[2]
    for p in range(rows // 2):
        blk = [
            oxl[...] * jnp.broadcast_to(cfb[b, 2 * p + c : 2 * p + c + 1, :], (SUB, count))
            for b in range(2) for c in range(2)
        ]
        lhs[4 * SUB * p : 4 * SUB * (p + 1), :] = join(blk, 0).astype(BF)


def place(lhs, w1, gbox):
    blocks, half, _ = gbox.shape
    for t in range(half // (2 * SUB)):
        o = dot(lhs[...], w1[:, 2 * LANES * t : 2 * LANES * (t + 1)])
        o = join([o[:, :LANES].reshape(blocks, SUB, LANES), o[:, LANES:].reshape(blocks, SUB, LANES)], 1)
        gbox[:, 2 * SUB * t : 2 * SUB * (t + 1), :] = o.astype(BF)


def apply_potential(first, count, gbox, pot, fya, fyb, fx, fxb, ya, yb, pk):
    half, grid = gbox.shape[1], pot.shape[1]
    wide = 3 * LANES
    planes = range(count)
    ls = []
    for d in planes:
        base = 4 * (first + d)
        for b in range(2):
            ls.append(join([gbox[base + 2 * b], gbox[base + 2 * b + 1]], 1))
    near = dot(join(ls, 0), fya[...]).astype(BF)
    far = dot(join([join([ls[2 * d], ls[2 * d + 1]], 1) for d in planes], 0), fyb[...]).astype(BF)
    cols = []
    for d in planes:
        a0 = near[2 * half * d : 2 * half * d + half]
        a2 = near[2 * half * d + half : 2 * half * (d + 1)]
        a1 = far[half * d : half * (d + 1)]
        for a in (a0, a1, a2):
            cols.append(join([a[:, :LANES], a[:, LANES:]], 0))
    psi = dot(fx[...], join(cols, 1))
    vs = []
    for d in planes:
        v = pot[first + d]
        v0, v1 = v[:, :LANES], v[:, LANES:]
        vs += [v0, join([v1, v1], 1), v0]
    vv = join(vs, 1)
    w = join([psi[:grid] * vv, psi[grid:] * vv], 0).astype(BF)
    bb = dot(fxb[...], w).astype(BF)
    p1, p2 = [], []
    for d in planes:
        def piece(j):
            sl = slice(wide * d + LANES * j, wide * d + LANES * (j + 1))
            return join([bb[:half, sl], bb[half:, sl]], 1)
        p1 += [piece(0), piece(2)]
        p2.append(piece(1))
    c1 = dot(join(p1, 0), ya[...])
    c2 = dot(join(p2, 0), yb[...])
    per_band = pk.shape[0] // 2
    for d in planes:
        for b in range(2):
            at = 2 * half * d + half * b
            cc = c1[at : at + half] + c2[half * d : half * (d + 1), 2 * LANES * b : 2 * LANES * (b + 1)]
            rows = [
                join([cc[SUB * h : SUB * (h + 1), LANES * c : LANES * (c + 1)] for h in range(half // SUB)], 1)
                for c in range(2)
            ]
            to = per_band * b + 2 * SUB * (first + d)
            pk[to : to + 2 * SUB, :] = join(rows, 0).astype(BF)


def pick(pk, w1t, oxl, out):
    rows = pk.shape[0]
    blocks = rows // SUB
    per_band = blocks // 2
    ones = (iota((blocks, rows), 1) // SUB == iota((blocks, rows), 0)).astype(F32).astype(BF)
    low = iota((per_band, LANES), 1) < LANES // 2
    step = 2 * LANES
    for t in range(w1t.shape[1] // step):
        sl = slice(step * t, step * (t + 1))
        d = dot(pk[...], w1t[:, sl])
        m = (d.reshape(blocks, SUB, step) * oxl[:, sl][None]).reshape(rows, step).astype(BF)
        s = dot(ones, m)
        for h in range(2):
            lanes = slice(LANES * h, LANES * (h + 1))
            d0, d1 = s[:per_band, lanes], s[per_band:, lanes]
            out[4 * t + 2 * h] = jnp.where(low, d0, pltpu.roll(d1, LANES // 2, 1)).astype(BF)
            out[4 * t + 2 * h + 1] = jnp.where(low, pltpu.roll(d0, LANES // 2, 1), d1).astype(BF)


def kernel(
    n_band, n_fft, coef_h, pot_h, col_h, len_h, orb_h, fz_h, fya_h, fyb_h, fx_h, fxb_h, ya_h, yb_h, fzb_h,
    applied, margin,
    coef, pot, q, length, orb, fz, fya, fyb, fx, fxb, ya, yb, fzb,
    w1, w1t, oxl, cfb, lhs, gbox, pk,
    send1, recv1, send2, recv2, send3, recv3, send4, recv4, send5, recv5,
    load_sem, fft_send, fft_recv, band_send, band_recv,
):
    loads = {}
    order = [
        (len_h, length.at[0])] + [
        (col_h.at[pl.ds(LANES * k, LANES)], q.at[k]) for k in range(q.shape[0])] + [
        (coef_h, coef), (fz_h, fz), (pot_h, pot), (fya_h, fya), (fyb_h, fyb), (fx_h, fx), (fxb_h, fxb),
        (ya_h, ya), (yb_h, yb), (orb_h, orb), (fzb_h, fzb)]
    for n, (src, dst) in enumerate(order):
        loads[n] = pltpu.make_async_copy(src, dst, load_sem.at[n])
        loads[n].start()
    nq = q.shape[0]

    barrier = pltpu.get_barrier_semaphore()
    for axis, n in (("fft", n_fft), ("band", n_band)):
        me = lax.axis_index(axis)
        for k in range(1, n):
            pl.semaphore_signal(
                barrier, inc=1, device_id={axis: lax.rem(me + k, n)}, device_id_type=MESH)
    exchanges = [
        Exchange("fft", n_fft, send1, recv1, fft_send.at[0], fft_recv.at[0]),
        Exchange("fft", n_fft, send2, recv2, fft_send.at[1], fft_recv.at[1]),
        Exchange("band", n_band, send3, recv3, band_send.at[0], band_recv.at[0]),
        Exchange("fft", n_fft, send4, recv4, fft_send.at[2], fft_recv.at[2]),
        Exchange("band", n_band, send5, recv5, band_send.at[1], band_recv.at[1]),
    ]

    bands, sticks, width = coef.shape
    half = width // 2
    for n in range(nq + 3):
        loads[n].wait()
    me = lax.axis_index("fft")
    row = jnp.sum(jnp.where(iota(q.shape, 0) == me // 2, q[...], 0), axis=0, keepdims=True)
    row = jnp.broadcast_to(row, (SUB, LANES))
    turned = pltpu.roll(row, sticks, 1)
    low = iota((SUB, LANES), 1) < sticks
    row = jnp.where(low == (lax.rem(me, 2) == 0), row, turned)
    x_freq = row // half
    y_freq = row - x_freq * half - half // 2
    x_freq = x_freq - half // 2
    size = join([length[...]] * bands, 1)
    size = jnp.broadcast_to(size, (SUB, LANES))
    below = size // 2
    which = iota((SUB, LANES), 0)
    rows = jnp.where(which == 0, -below, jnp.where(which == 1, size - below, x_freq * x_freq + y_freq * y_freq))
    down = rows.astype(F32).T
    z_freq = iota((bands * sticks, width), 1)
    z_freq = (jnp.where(z_freq >= half, z_freq - half, z_freq) - half // 2).astype(F32)
    live = (z_freq >= down[:, 0:1]) & (z_freq < down[:, 1:2])
    masked = jnp.where(live, coef[...].reshape(bands * sticks, width), 0.0)
    high = masked.astype(BF)
    rest = (masked - high.astype(F32)).astype(BF)
    columns = dot_t(fz[0], high) + (dot_t(fz[0], rest) + dot_t(fz[1], high))
    send1[...] = columns.reshape(send1.shape).astype(BF)
    pl.semaphore_wait(barrier, n_fft + n_band - 2)
    exchanges[0].start()

    build_cells(half, q, w1, w1t, oxl)
    for n in range(nq + 3, len(order)):
        loads[n].wait()
    exchanges[0].wait()

    spread_sticks(recv1, oxl, cfb, lhs)
    place(lhs, w1, gbox)
    count = 4
    for first in range(0, pot.shape[0], count):
        apply_potential(first, count, gbox, pot, fya, fyb, fx, fxb, ya, yb, pk)
    pick(pk, w1t, oxl, send2)
    exchanges[1].start()

    exchanges[1].wait()

    values = recv2[...].reshape(-1, bands * sticks)
    local = (dot(fzb[0], values) + dot(fzb[1], values)).T
    kinetic = (down[:, 2:3] + z_freq * z_freq) * (2.0 / (half * half))
    h = jnp.where(live, kinetic * masked + local, 0.0)
    group = sticks // n_band
    for r in range(n_band):
        one, two = r * group, sticks + r * group
        send3[r] = join([h[one : one + group], h[two : two + group]], 0).astype(BF)
    exchanges[2].start()
    applied[...] = h.astype(BF).reshape(applied.shape)
    exchanges[2].wait()

    ours = recv3[...].astype(F32).reshape(n_band * bands, group, width)
    both = join([ours, join([ours[:, :, half:], -ours[:, :, :half]], 2)], 0)
    total = None
    for j in range(group):
        term = dot(both[:, j, :].astype(BF), orb[j])
        total = term if total is None else total + term
    total = total.T
    per = total.shape[0] // (n_band * n_fft)
    total = total.reshape(n_band, n_fft * per, total.shape[1])
    total = join([total[r] for r in range(n_band)], 1)
    for f in range(n_fft):
        send4[f] = total[per * f : per * (f + 1)]
    exchanges[3].start()
    exchanges[3].wait()
    total = recv4[0]
    for f in range(1, n_fft):
        total = total + recv4[f]
    cols = margin.shape[1]
    for r in range(n_band):
        send5[r] = total[:, cols * r : cols * (r + 1)]
    exchanges[4].start()
    exchanges[4].wait()
    total = recv5[0]
    for r in range(1, n_band):
        total = total + recv5[r]
    margin[...] = total


def per_device(n_band, n_fft, band_coeffs, potential, stick_column, stick_length, orbitals):
    bands, sticks, width = band_coeffs.shape
    half = width // 2
    planes, grid = potential.shape[:2]
    rows = orbitals.shape[0]
    orbitals = orbitals.transpose(1, 2, 0)
    tables = dft_tables(half, grid)
    count, group = stick_column.shape[0], orbitals.shape[0]
    per = rows // (n_band * n_fft)
    cells = half // SUB * LANES
    blocks = planes * bands * 2
    first = (n_fft, 2 * planes, bands * sticks)
    swap = (n_band, bands * group, width)
    cols = 2 * n_band * bands
    fold = (n_fft, per, n_band * cols)
    last = (n_band, per, cols)
    vm, sem = pltpu.VMEM, pltpu.SemaphoreType.DMA
    n_rows = count // LANES
    return pl.pallas_call(
        functools.partial(kernel, n_band, n_fft),
        out_shape=(
            jax.ShapeDtypeStruct(band_coeffs.shape, BF), jax.ShapeDtypeStruct((per, cols), F32)),
        in_specs=[pl.BlockSpec(memory_space=pl.ANY)] * 13,
        out_specs=(pl.BlockSpec(memory_space=pltpu.VMEM),) * 2,
        scratch_shapes=[
            vm(band_coeffs.shape, F32), vm(potential.shape, F32), vm((n_rows, LANES), I32),
            vm((1, sticks), I32), vm(orbitals.shape, BF)]
        + [vm(t.shape, BF) for t in tables]
        + [
            vm((count, cells), BF), vm((cells, count), BF), vm((SUB, count), F32),
            vm((bands, 2 * planes, count), F32), vm((SUB * blocks, count), BF),
            vm((blocks, half, LANES), BF), vm((SUB * blocks, cells), BF)]
        + [vm(first, BF)] * 4 + [vm(swap, BF)] * 2 + [vm(fold, F32)] * 2 + [vm(last, F32)] * 2
        + [sem((n_rows + 12,)), sem((3, n_fft)), sem((3, n_fft)), sem((2, n_band)), sem((2, n_band))],
        compiler_params=pltpu.CompilerParams(
            collective_id=0, has_side_effects=True, vmem_limit_bytes=60 * 1024 * 1024),
        name="hamiltonian",
    )(band_coeffs, potential, stick_column, stick_length, orbitals, *[jnp.asarray(t) for t in tables])


def solution(mesh):
    placed = (
        P("band", "fft", None),
        P("fft", None, None),
        P(),
        P("fft"),
        P(None, ("band", "fft"), None),
    )
    return jax.shard_map(
        functools.partial(per_device, mesh.shape["band"], mesh.shape["fft"]),
        mesh=mesh,
        in_specs=placed,
        out_specs=(P("band", "fft", None), P(("band", "fft"), None)),
        check_vma=False,
    )
```

```python
import functools
import math

import jax
import jax.numpy as jnp
import numpy as np
from jax import lax
from jax.experimental import pallas as pl
from jax.experimental.pallas import tpu as pltpu
from jax.sharding import PartitionSpec as P

BF = jnp.bfloat16
F32 = jnp.float32
I32 = jnp.int32
MESH = pl.DeviceIdType.MESH
LANES = 128
SUB = 8


def dft_tables(half, grid):
    freq = np.arange(half) - half // 2
    angle = (freq[:, None] * np.arange(grid)[None, :] % grid) * (2.0 * math.pi / grid)
    co, si = np.cos(angle), np.sin(angle)
    cp, sp = (np.concatenate([a, np.zeros((LANES - half, grid))], 0) for a in (co, si))
    near, far = slice(0, LANES), slice(LANES, grid)

    def ahead(part):
        return (np.concatenate([cp[:, part], -sp[:, part]], 0),
                np.concatenate([sp[:, part], cp[:, part]], 0))

    def back(part):
        return (np.concatenate([cp[:, part].T, -sp[:, part].T], 1),
                np.concatenate([sp[:, part].T, cp[:, part].T], 1))

    y_near = np.concatenate(ahead(near), 1)
    r, i = ahead(far)
    o = np.zeros_like(r)
    y_far = np.concatenate([np.concatenate([r, o, i, o], 1), np.concatenate([o, r, o, i], 1)], 0)
    order = np.concatenate([np.arange(0, half, 2), np.arange(1, half, 2)])
    cx, sx = co[order], si[order]
    x_ahead = np.concatenate(
        [np.concatenate([cx.T, -sx.T], 1), np.concatenate([sx.T, cx.T], 1)], 0)
    parts = []
    for part in (slice(0, half // 2), slice(half // 2, half)):
        c, s = cx[part, : grid // 2], sx[part, : grid // 2]
        parts.append(np.concatenate([np.concatenate([c, s], 1), np.concatenate([-s, c], 1)], 0))
    x_back = np.stack(parts)
    yb_near = np.concatenate(back(near), 0)
    r, i = back(far)
    o = np.zeros_like(r)
    yb_far = np.concatenate([np.concatenate([r, o, i, o], 0), np.concatenate([o, r, o, i], 0)], 1)
    z_ahead = np.stack(
        [np.concatenate([co.T, -si.T], 1), np.concatenate([si.T, co.T], 1)], 1
    ).reshape(2 * grid, 2 * half)
    z_back = np.concatenate(
        [np.stack([co, si], -1).reshape(half, -1), np.stack([-si, co], -1).reshape(half, -1)], 0
    ) / float(grid) ** 3

    def two_part(a):
        high = a.astype(np.float32).astype(BF)
        low = (a - high.astype(np.float64)).astype(np.float32).astype(BF)
        return np.stack([high, low])

    plain = [a.astype(np.float32).astype(BF) for a in (y_near, y_far, x_ahead, x_back, yb_near, yb_far)]
    return [two_part(z_ahead)] + plain + [two_part(z_back)]


def dot(a, b):
    return jnp.dot(a, b, preferred_element_type=F32)


def dot_t(a, b):
    return lax.dot_general(a, b, (((1,), (1,)), ((), ())), preferred_element_type=F32)


def iota(shape, dim):
    return lax.broadcasted_iota(I32, shape, dim)


def join(parts, axis):
    return jnp.concatenate(parts, axis=axis)


class Exchange:
    def __init__(self, axis, n, src, dst, send_sem, recv_sem):
        me = lax.axis_index(axis)
        self.copies = []
        for k in range(1, n):
            peer = lax.rem(me + k, n)
            self.copies.append(pltpu.make_async_remote_copy(
                src_ref=src.at[peer], dst_ref=dst.at[me],
                send_sem=send_sem.at[k], recv_sem=recv_sem.at[k],
                device_id={axis: peer}, device_id_type=MESH))
        self.own = pltpu.make_async_copy(src.at[me], dst.at[me], send_sem.at[0])

    def start(self):
        for copy in self.copies:
            copy.start()
        self.own.start()

    def wait(self):
        self.own.wait()
        for copy in self.copies:
            copy.wait()


def build_cells(half, q, w1, w1t, oxl):
    qq = q[...]
    xs = qq // half
    ys = qq - xs * half
    xs = lax.rem(xs, 2) * (half // 2) + xs // 2
    xh = xs // SUB
    xl = xs - xh * SUB
    cell = xh * LANES + ys
    down = cell.astype(F32).T
    cells, rows = w1t.shape[0], qq.shape[0]
    for k in range(rows):
        sl = slice(LANES * k, LANES * (k + 1))
        w1t[:, sl] = (iota((cells, LANES), 0) == cell[k : k + 1, :]).astype(F32).astype(BF)
        w1[sl, :] = (iota((LANES, cells), 1).astype(F32) == down[:, k : k + 1]).astype(F32).astype(BF)
        oxl[:, sl] = (iota((SUB, LANES), 0) == xl[k : k + 1, :]).astype(F32)


def spread_sticks(recv, oxl, cfb, lhs):
    nf, rows, lanes = recv.shape
    low = iota((rows, lanes), 1) < lanes // 2
    for k in range(nf // 2):
        a = recv[2 * k].astype(F32)
        b = recv[2 * k + 1].astype(F32)
        sl = slice(lanes * k, lanes * (k + 1))
        cfb[0, :, sl] = jnp.where(low, a, pltpu.roll(b, lanes // 2, 1))
        cfb[1, :, sl] = jnp.where(low, pltpu.roll(a, lanes // 2, 1), b)
    count = cfb.shape[2]
    for p in range(rows // 2):
        blk = [
            oxl[...] * jnp.broadcast_to(cfb[b, 2 * p + c : 2 * p + c + 1, :], (SUB, count))
            for b in range(2) for c in range(2)
        ]
        lhs[4 * SUB * p : 4 * SUB * (p + 1), :] = join(blk, 0).astype(BF)


def place(lhs, w1, gbox):
    blocks, half, _ = gbox.shape
    for t in range(half // (2 * SUB)):
        o = dot(lhs[...], w1[:, 2 * LANES * t : 2 * LANES * (t + 1)])
        o = join([o[:, :LANES].reshape(blocks, SUB, LANES), o[:, LANES:].reshape(blocks, SUB, LANES)], 1)
        gbox[:, 2 * SUB * t : 2 * SUB * (t + 1), :] = o.astype(BF)


def apply_potential(first, count, gbox, pot, fya, fyb, fx, fxb, ya, yb, pk):
    half, grid = gbox.shape[1], pot.shape[1]
    wide = 3 * LANES
    planes = range(count)
    ls = []
    for d in planes:
        base = 4 * (first + d)
        for b in range(2):
            ls.append(join([gbox[base + 2 * b], gbox[base + 2 * b + 1]], 1))
    near = dot(join(ls, 0), fya[...]).astype(BF)
    far = dot(join([join([ls[2 * d], ls[2 * d + 1]], 1) for d in planes], 0), fyb[...]).astype(BF)
    cols = []
    for d in planes:
        a0 = near[2 * half * d : 2 * half * d + half]
        a2 = near[2 * half * d + half : 2 * half * (d + 1)]
        a1 = far[half * d : half * (d + 1)]
        for a in (a0, a1, a2):
            cols.append(join([a[:, :LANES], a[:, LANES:]], 0))
    psi = dot(fx[...], join(cols, 1))
    vs = []
    for d in planes:
        v = pot[first + d]
        v0, v1 = v[:, :LANES], v[:, LANES:]
        vs += [v0, join([v1, v1], 1), v0]
    vv = join(vs, 1)
    re, im = psi[:grid] * vv, psi[grid:] * vv
    mid, quarter = grid // 2, half // 2
    even = dot(fxb[0], join([re[:mid] + re[mid:], im[:mid] + im[mid:]], 0).astype(BF))
    odd = dot(fxb[1], join([re[:mid] - re[mid:], im[:mid] - im[mid:]], 0).astype(BF))
    bb = join([even[:quarter], odd[:quarter], even[quarter:], odd[quarter:]], 0).astype(BF)
    p1, p2 = [], []
    for d in planes:
        def piece(j):
            sl = slice(wide * d + LANES * j, wide * d + LANES * (j + 1))
            return join([bb[:half, sl], bb[half:, sl]], 1)
        p1 += [piece(0), piece(2)]
        p2.append(piece(1))
    c1 = dot(join(p1, 0), ya[...])
    c2 = dot(join(p2, 0), yb[...])
    per_band = pk.shape[0] // 2
    for d in planes:
        for b in range(2):
            at = 2 * half * d + half * b
            cc = c1[at : at + half] + c2[half * d : half * (d + 1), 2 * LANES * b : 2 * LANES * (b + 1)]
            rows = [
                join([cc[SUB * h : SUB * (h + 1), LANES * c : LANES * (c + 1)] for h in range(half // SUB)], 1)
                for c in range(2)
            ]
            to = per_band * b + 2 * SUB * (first + d)
            pk[to : to + 2 * SUB, :] = join(rows, 0).astype(BF)


def pick(pk, w1t, oxl, kept, out):
    rows = pk.shape[0]
    blocks = rows // SUB
    per_band = blocks // 2
    ones = (iota((blocks, rows), 1) // SUB == iota((blocks, rows), 0)).astype(F32).astype(BF)
    low = iota((per_band, LANES), 1) < LANES // 2
    step = 2 * LANES
    for t in range(w1t.shape[1] // step):
        sl = slice(step * t, step * (t + 1))
        d = dot(pk[...], w1t[:, sl])
        kept[:, sl] = (d.reshape(blocks, SUB, step) * oxl[:, sl][None]).reshape(rows, step).astype(BF)
    s = dot(ones, kept[...])
    for h in range(out.shape[0] // 2):
        lanes = slice(LANES * h, LANES * (h + 1))
        d0, d1 = s[:per_band, lanes], s[per_band:, lanes]
        out[2 * h] = jnp.where(low, d0, pltpu.roll(d1, LANES // 2, 1)).astype(BF)
        out[2 * h + 1] = jnp.where(low, pltpu.roll(d0, LANES // 2, 1), d1).astype(BF)


def kernel(
    n_band, n_fft, coef_h, pot_h, col_h, len_h, orb_h, fz_h, fya_h, fyb_h, fx_h, fxb_h, ya_h, yb_h, fzb_h,
    applied, margin,
    coef, pot, q, length, orb, fz, fya, fyb, fx, fxb, ya, yb, fzb,
    w1, w1t, oxl, cfb, lhs, gbox, pk,
    send1, recv1, send2, recv2, send3, recv3, send4, recv4, send5, recv5,
    load_sem, fft_send, fft_recv, band_send, band_recv,
):
    barrier = pltpu.get_barrier_semaphore()
    for axis, n in (("fft", n_fft), ("band", n_band)):
        me = lax.axis_index(axis)
        for k in range(1, n):
            pl.semaphore_signal(
                barrier, inc=1, device_id={axis: lax.rem(me + k, n)}, device_id_type=MESH)
    loads = {}
    order = [
        (len_h, length.at[0])] + [
        (col_h.at[pl.ds(LANES * k, LANES)], q.at[k]) for k in range(q.shape[0])] + [
        (coef_h, coef), (fz_h, fz), (pot_h, pot), (fya_h, fya), (fyb_h, fyb), (fx_h, fx), (fxb_h, fxb),
        (ya_h, ya), (yb_h, yb), (orb_h, orb), (fzb_h, fzb)]
    for n, (src, dst) in enumerate(order):
        loads[n] = pltpu.make_async_copy(src, dst, load_sem.at[n])
        loads[n].start()
    nq = q.shape[0]

    exchanges = [
        Exchange("fft", n_fft, send1, recv1, fft_send.at[0], fft_recv.at[0]),
        Exchange("fft", n_fft, send2, recv2, fft_send.at[1], fft_recv.at[1]),
        Exchange("band", n_band, send3, recv3, band_send.at[0], band_recv.at[0]),
        Exchange("fft", n_fft, send4, recv4, fft_send.at[2], fft_recv.at[2]),
        Exchange("band", n_band, send5, recv5, band_send.at[1], band_recv.at[1]),
    ]

    bands, sticks, width = coef.shape
    half = width // 2
    for n in range(nq + 3):
        loads[n].wait()
    me = lax.axis_index("fft")
    row = jnp.sum(jnp.where(iota(q.shape, 0) == me // 2, q[...], 0), axis=0, keepdims=True)
    row = jnp.broadcast_to(row, (SUB, LANES))
    turned = pltpu.roll(row, sticks, 1)
    low = iota((SUB, LANES), 1) < sticks
    row = jnp.where(low == (lax.rem(me, 2) == 0), row, turned)
    x_freq = row // half
    y_freq = row - x_freq * half - half // 2
    x_freq = x_freq - half // 2
    size = join([length[...]] * bands, 1)
    size = jnp.broadcast_to(size, (SUB, LANES))
    below = size // 2
    which = iota((SUB, LANES), 0)
    rows = jnp.where(which == 0, -below, jnp.where(which == 1, size - below, x_freq * x_freq + y_freq * y_freq))
    down = rows.astype(F32).T
    z_freq = iota((bands * sticks, width), 1)
    z_freq = (jnp.where(z_freq >= half, z_freq - half, z_freq) - half // 2).astype(F32)
    live = (z_freq >= down[:, 0:1]) & (z_freq < down[:, 1:2])
    masked = jnp.where(live, coef[...].reshape(bands * sticks, width), 0.0)
    high = masked.astype(BF)
    rest = (masked - high.astype(F32)).astype(BF)
    columns = dot_t(fz[0], high) + (dot_t(fz[0], rest) + dot_t(fz[1], high))
    send1[...] = columns.reshape(send1.shape).astype(BF)
    pl.semaphore_wait(barrier, n_fft + n_band - 2)
    exchanges[0].start()

    build_cells(half, q, w1, w1t, oxl)
    for n in range(nq + 3, len(order)):
        loads[n].wait()
    exchanges[0].wait()

    spread_sticks(recv1, oxl, cfb, lhs)
    place(lhs, w1, gbox)
    count = 4
    for first in range(0, pot.shape[0], count):
        apply_potential(first, count, gbox, pot, fya, fyb, fx, fxb, ya, yb, pk)
    pick(pk, w1t, oxl, lhs, send2)
    exchanges[1].start()

    exchanges[1].wait()

    values = recv2[...].reshape(-1, bands * sticks)
    local = (dot(fzb[0], values) + dot(fzb[1], values)).T
    kinetic = (down[:, 2:3] + z_freq * z_freq) * (2.0 / (half * half))
    h = jnp.where(live, kinetic * masked + local, 0.0)
    group = sticks // n_band
    for r in range(n_band):
        one, two = r * group, sticks + r * group
        a, b = h[one : one + group], h[two : two + group]
        tail = join([a[:, LANES:], b[:, LANES:]], 1)
        send3[r] = join([a[:, :LANES], b[:, :LANES], tail], 0).astype(BF)
    exchanges[2].start()
    applied[...] = h.astype(BF).reshape(applied.shape)
    exchanges[2].wait()

    ours = recv3[...].astype(F32)
    tail = ours[:, 2 * group :]
    ours = join([
        join([ours[:, :group], tail[:, :, : width - LANES]], 2)[:, None],
        join([ours[:, group : 2 * group], tail[:, :, width - LANES :]], 2)[:, None]], 1)
    ours = ours.reshape(n_band * bands, group, width)
    both = join([ours, join([ours[:, :, half:], -ours[:, :, :half]], 2)], 0)
    total = None
    for j in range(group):
        term = dot(both[:, j, :].astype(BF), orb[j])
        total = term if total is None else total + term
    total = total.T
    per = total.shape[0] // (n_band * n_fft)
    total = total.reshape(n_band, n_fft * per, total.shape[1])
    total = join([total[r] for r in range(n_band)], 1)
    for f in range(n_fft):
        send4[f] = total[per * f : per * (f + 1)]
    exchanges[3].start()
    exchanges[3].wait()
    total = recv4[0]
    for f in range(1, n_fft):
        total = total + recv4[f]
    cols = margin.shape[1]
    for r in range(n_band):
        send5[r] = total[:, cols * r : cols * (r + 1)]
    exchanges[4].start()
    exchanges[4].wait()
    total = recv5[0]
    for r in range(1, n_band):
        total = total + recv5[r]
    margin[...] = total


def per_device(n_band, n_fft, band_coeffs, potential, stick_column, stick_length, orbitals):
    bands, sticks, width = band_coeffs.shape
    half = width // 2
    planes, grid = potential.shape[:2]
    rows = orbitals.shape[0]
    orbitals = orbitals.transpose(1, 2, 0)
    tables = dft_tables(half, grid)
    count, group = stick_column.shape[0], orbitals.shape[0]
    per = rows // (n_band * n_fft)
    cells = half // SUB * LANES
    blocks = planes * bands * 2
    first = (n_fft, 2 * planes, bands * sticks)
    swap = (n_band, bands * group * width // LANES, LANES)
    cols = 2 * n_band * bands
    fold = (n_fft, per, n_band * cols)
    last = (n_band, per, cols)
    vm, sem = pltpu.VMEM, pltpu.SemaphoreType.DMA
    n_rows = count // LANES
    return pl.pallas_call(
        functools.partial(kernel, n_band, n_fft),
        out_shape=(
            jax.ShapeDtypeStruct(band_coeffs.shape, BF), jax.ShapeDtypeStruct((per, cols), F32)),
        in_specs=[pl.BlockSpec(memory_space=pl.ANY)] * 13,
        out_specs=(pl.BlockSpec(memory_space=pltpu.VMEM),) * 2,
        scratch_shapes=[
            vm(band_coeffs.shape, F32), vm(potential.shape, F32), vm((n_rows, LANES), I32),
            vm((1, sticks), I32), vm(orbitals.shape, BF)]
        + [vm(t.shape, BF) for t in tables]
        + [
            vm((count, cells), BF), vm((cells, count), BF), vm((SUB, count), F32),
            vm((bands, 2 * planes, count), F32), vm((SUB * blocks, count), BF),
            vm((blocks, half, LANES), BF), vm((SUB * blocks, cells), BF)]
        + [vm(first, BF)] * 4 + [vm(swap, BF)] * 2 + [vm(fold, F32)] * 2 + [vm(last, F32)] * 2
        + [sem((n_rows + 12,)), sem((3, n_fft)), sem((3, n_fft)), sem((2, n_band)), sem((2, n_band))],
        compiler_params=pltpu.CompilerParams(
            collective_id=0, has_side_effects=True, vmem_limit_bytes=60 * 1024 * 1024),
        name="hamiltonian",
    )(band_coeffs, potential, stick_column, stick_length, orbitals, *[jnp.asarray(t) for t in tables])


def solution(mesh):
    placed = (
        P("band", "fft", None),
        P("fft", None, None),
        P(),
        P("fft"),
        P(None, ("band", "fft"), None),
    )
    return jax.shard_map(
        functools.partial(per_device, mesh.shape["band"], mesh.shape["fft"]),
        mesh=mesh,
        in_specs=placed,
        out_specs=(P("band", "fft", None), P(("band", "fft"), None)),
        check_vma=False,
    )
```

```python
import functools
import math

import jax
import jax.numpy as jnp
import numpy as np
from jax import lax
from jax.experimental import pallas as pl
from jax.experimental.pallas import tpu as pltpu
from jax.sharding import PartitionSpec as P

BF = jnp.bfloat16
F32 = jnp.float32
I32 = jnp.int32
MESH = pl.DeviceIdType.MESH
LANES = 128
SUB = 8


def dft_tables(half, grid):
    freq = np.arange(half) - half // 2
    angle = (freq[:, None] * np.arange(grid)[None, :] % grid) * (2.0 * math.pi / grid)
    co, si = np.cos(angle), np.sin(angle)
    cp, sp = (np.concatenate([a, np.zeros((LANES - half, grid))], 0) for a in (co, si))
    near, far = slice(0, LANES), slice(LANES, grid)

    def ahead(part):
        return (np.concatenate([cp[:, part], -sp[:, part]], 0),
                np.concatenate([sp[:, part], cp[:, part]], 0))

    def back(part):
        return (np.concatenate([cp[:, part].T, -sp[:, part].T], 1),
                np.concatenate([sp[:, part].T, cp[:, part].T], 1))

    y_near = np.concatenate(ahead(near), 1)
    r, i = ahead(far)
    o = np.zeros_like(r)
    y_far = np.concatenate([np.concatenate([r, o, i, o], 1), np.concatenate([o, r, o, i], 1)], 0)
    order = np.concatenate([np.arange(0, half, 2), np.arange(1, half, 2)])
    cx, sx = co[order], si[order]
    x_ahead = np.concatenate(
        [np.concatenate([cx.T, -sx.T], 1), np.concatenate([sx.T, cx.T], 1)], 0)
    parts = []
    for part in (slice(0, half // 2), slice(half // 2, half)):
        c, s = cx[part, : grid // 2], sx[part, : grid // 2]
        parts.append(np.concatenate([np.concatenate([c, s], 1), np.concatenate([-s, c], 1)], 0))
    x_back = np.stack(parts)
    yb_near = np.concatenate(back(near), 0)
    r, i = back(far)
    o = np.zeros_like(r)
    yb_far = np.concatenate([np.concatenate([r, o, i, o], 0), np.concatenate([o, r, o, i], 0)], 1)
    z_ahead = np.stack(
        [np.concatenate([co.T, -si.T], 1), np.concatenate([si.T, co.T], 1)], 1
    ).reshape(2 * grid, 2 * half)
    z_back = np.concatenate(
        [np.stack([co, si], -1).reshape(half, -1), np.stack([-si, co], -1).reshape(half, -1)], 0
    ) / float(grid) ** 3

    def two_part(a):
        high = a.astype(np.float32).astype(BF)
        low = (a - high.astype(np.float64)).astype(np.float32).astype(BF)
        return np.stack([high, low])

    plain = [a.astype(np.float32).astype(BF) for a in (y_near, y_far, x_ahead, x_back, yb_near, yb_far)]
    return [two_part(z_ahead)] + plain + [two_part(z_back)]


def dot(a, b):
    return jnp.dot(a, b, preferred_element_type=F32)


def dot_t(a, b):
    return lax.dot_general(a, b, (((1,), (1,)), ((), ())), preferred_element_type=F32)


def iota(shape, dim):
    return lax.broadcasted_iota(I32, shape, dim)


def join(parts, axis):
    return jnp.concatenate(parts, axis=axis)


class Exchange:
    def __init__(self, axis, n, src, dst, send_sem, recv_sem):
        me = lax.axis_index(axis)
        self.copies = []
        for k in range(1, n):
            peer = lax.rem(me + k, n)
            self.copies.append(pltpu.make_async_remote_copy(
                src_ref=src.at[peer], dst_ref=dst.at[me],
                send_sem=send_sem.at[k], recv_sem=recv_sem.at[k],
                device_id={axis: peer}, device_id_type=MESH))
        self.own = pltpu.make_async_copy(src.at[me], dst.at[me], send_sem.at[0])

    def start(self):
        for copy in self.copies:
            copy.start()
        self.own.start()

    def wait(self):
        self.own.wait()
        for copy in self.copies:
            copy.wait()


def build_cells(half, q, w1, w1t, oxl):
    qq = q[...]
    xs = qq // half
    ys = qq - xs * half
    xs = lax.rem(xs, 2) * (half // 2) + xs // 2
    xh = xs // SUB
    xl = xs - xh * SUB
    cell = xh * LANES + ys
    down = cell.astype(F32).T
    cells, rows = w1t.shape[0], qq.shape[0]
    for k in range(rows):
        sl = slice(LANES * k, LANES * (k + 1))
        w1t[:, sl] = (iota((cells, LANES), 0) == cell[k : k + 1, :]).astype(F32).astype(BF)
        w1[sl, :] = (iota((LANES, cells), 1).astype(F32) == down[:, k : k + 1]).astype(F32).astype(BF)
        oxl[:, sl] = (iota((SUB, LANES), 0) == xl[k : k + 1, :]).astype(F32)


def spread_sticks(recv, oxl, cfb, lhs):
    nf, rows, lanes = recv.shape
    low = iota((rows, lanes), 1) < lanes // 2
    for k in range(nf // 2):
        a = recv[2 * k].astype(F32)
        b = recv[2 * k + 1].astype(F32)
        sl = slice(lanes * k, lanes * (k + 1))
        cfb[0, :, sl] = jnp.where(low, a, pltpu.roll(b, lanes // 2, 1))
        cfb[1, :, sl] = jnp.where(low, pltpu.roll(a, lanes // 2, 1), b)
    count = cfb.shape[2]
    for p in range(rows // 2):
        blk = [
            oxl[...] * jnp.broadcast_to(cfb[b, 2 * p + c : 2 * p + c + 1, :], (SUB, count))
            for b in range(2) for c in range(2)
        ]
        lhs[4 * SUB * p : 4 * SUB * (p + 1), :] = join(blk, 0).astype(BF)


def place(lhs, w1, gbox):
    blocks, half, _ = gbox.shape
    for t in range(half // (2 * SUB)):
        o = dot(lhs[...], w1[:, 2 * LANES * t : 2 * LANES * (t + 1)])
        o = join([o[:, :LANES].reshape(blocks, SUB, LANES), o[:, LANES:].reshape(blocks, SUB, LANES)], 1)
        gbox[:, 2 * SUB * t : 2 * SUB * (t + 1), :] = o.astype(BF)


def apply_potential(first, count, gbox, pot, fya, fyb, fx, fxb, ya, yb, pk):
    half, grid = gbox.shape[1], pot.shape[1]
    wide = 3 * LANES
    planes = range(count)
    ls = []
    for d in planes:
        base = 4 * (first + d)
        for b in range(2):
            ls.append(join([gbox[base + 2 * b], gbox[base + 2 * b + 1]], 1))
    near = dot(join(ls, 0), fya[...]).astype(BF)
    far = dot(join([join([ls[2 * d], ls[2 * d + 1]], 1) for d in planes], 0), fyb[...]).astype(BF)
    cols = []
    for d in planes:
        a0 = near[2 * half * d : 2 * half * d + half]
        a2 = near[2 * half * d + half : 2 * half * (d + 1)]
        a1 = far[half * d : half * (d + 1)]
        for a in (a0, a1, a2):
            cols.append(join([a[:, :LANES], a[:, LANES:]], 0))
    psi = dot(fx[...], join(cols, 1))
    vs = []
    for d in planes:
        v = pot[first + d]
        v0, v1 = v[:, :LANES], v[:, LANES:]
        vs += [v0, join([v1, v1], 1), v0]
    vv = join(vs, 1)
    re, im = psi[:grid] * vv, psi[grid:] * vv
    mid, quarter = grid // 2, half // 2
    even = dot(fxb[0], join([re[:mid] + re[mid:], im[:mid] + im[mid:]], 0).astype(BF))
    odd = dot(fxb[1], join([re[:mid] - re[mid:], im[:mid] - im[mid:]], 0).astype(BF))
    bb = join([even[:quarter], odd[:quarter], even[quarter:], odd[quarter:]], 0).astype(BF)
    p1, p2 = [], []
    for d in planes:
        def piece(j):
            sl = slice(wide * d + LANES * j, wide * d + LANES * (j + 1))
            return join([bb[:half, sl], bb[half:, sl]], 1)
        p1 += [piece(0), piece(2)]
        p2.append(piece(1))
    c1 = dot(join(p1, 0), ya[...])
    c2 = dot(join(p2, 0), yb[...])
    per_band = pk.shape[0] // 2
    for d in planes:
        for b in range(2):
            at = 2 * half * d + half * b
            cc = c1[at : at + half] + c2[half * d : half * (d + 1), 2 * LANES * b : 2 * LANES * (b + 1)]
            rows = [
                join([cc[SUB * h : SUB * (h + 1), LANES * c : LANES * (c + 1)] for h in range(half // SUB)], 1)
                for c in range(2)
            ]
            to = per_band * b + 2 * SUB * (first + d)
            pk[to : to + 2 * SUB, :] = join(rows, 0).astype(BF)


def pick(pk, w1t, oxl, kept, out):
    rows = pk.shape[0]
    blocks = rows // SUB
    per_band = blocks // 2
    ones = (iota((blocks, rows), 1) // SUB == iota((blocks, rows), 0)).astype(F32).astype(BF)
    low = iota((per_band, LANES), 1) < LANES // 2
    step = 2 * LANES
    for t in range(w1t.shape[1] // step):
        sl = slice(step * t, step * (t + 1))
        d = dot(pk[...], w1t[:, sl])
        kept[:, sl] = (d.reshape(blocks, SUB, step) * oxl[:, sl][None]).reshape(rows, step).astype(BF)
    s = dot(ones, kept[...])
    for h in range(out.shape[0] // 2):
        lanes = slice(LANES * h, LANES * (h + 1))
        d0, d1 = s[:per_band, lanes], s[per_band:, lanes]
        out[2 * h] = jnp.where(low, d0, pltpu.roll(d1, LANES // 2, 1)).astype(BF)
        out[2 * h + 1] = jnp.where(low, pltpu.roll(d0, LANES // 2, 1), d1).astype(BF)


def kernel(
    n_band, n_fft, coef_h, pot_h, col_h, len_h, orb_h, fz_h, fya_h, fyb_h, fx_h, fxb_h, ya_h, yb_h, fzb_h,
    applied, margin,
    coef, pot, q, length, orb, fz, fya, fyb, fx, fxb, ya, yb, fzb,
    w1, w1t, oxl, cfb, lhs, gbox, pk,
    send1, recv1, send2, recv2, send3, recv3, send4, recv4, send5, recv5,
    kept_h, out_sem, load_sem, fft_send, fft_recv, band_send, band_recv,
):
    barrier = pltpu.get_barrier_semaphore()
    for axis, n in (("fft", n_fft), ("band", n_band)):
        me = lax.axis_index(axis)
        for k in range(1, n):
            pl.semaphore_signal(
                barrier, inc=1, device_id={axis: lax.rem(me + k, n)}, device_id_type=MESH)
    loads = {}
    order = [
        (len_h, length.at[0])] + [
        (col_h.at[pl.ds(LANES * k, LANES)], q.at[k]) for k in range(q.shape[0])] + [
        (coef_h, coef), (fz_h, fz), (pot_h, pot), (fya_h, fya), (fyb_h, fyb), (fx_h, fx), (fxb_h, fxb),
        (ya_h, ya), (yb_h, yb), (orb_h, orb), (fzb_h, fzb)]
    for n, (src, dst) in enumerate(order):
        loads[n] = pltpu.make_async_copy(src, dst, load_sem.at[n])
        loads[n].start()
    nq = q.shape[0]

    exchanges = [
        Exchange("fft", n_fft, send1, recv1, fft_send.at[0], fft_recv.at[0]),
        Exchange("fft", n_fft, send2, recv2, fft_send.at[1], fft_recv.at[1]),
        Exchange("band", n_band, send3, recv3, band_send.at[0], band_recv.at[0]),
        Exchange("fft", n_fft, send4, recv4, fft_send.at[2], fft_recv.at[2]),
        Exchange("band", n_band, send5, recv5, band_send.at[1], band_recv.at[1]),
    ]

    bands, sticks, width = coef.shape
    half = width // 2
    for n in range(nq + 3):
        loads[n].wait()
    me = lax.axis_index("fft")
    row = jnp.sum(jnp.where(iota(q.shape, 0) == me // 2, q[...], 0), axis=0, keepdims=True)
    row = jnp.broadcast_to(row, (SUB, LANES))
    turned = pltpu.roll(row, sticks, 1)
    low = iota((SUB, LANES), 1) < sticks
    row = jnp.where(low == (lax.rem(me, 2) == 0), row, turned)
    x_freq = row // half
    y_freq = row - x_freq * half - half // 2
    x_freq = x_freq - half // 2
    size = join([length[...]] * bands, 1)
    size = jnp.broadcast_to(size, (SUB, LANES))
    below = size // 2
    which = iota((SUB, LANES), 0)
    rows = jnp.where(which == 0, -below, jnp.where(which == 1, size - below, x_freq * x_freq + y_freq * y_freq))
    down = rows.astype(F32).T
    z_freq = iota((bands * sticks, width), 1)
    z_freq = (jnp.where(z_freq >= half, z_freq - half, z_freq) - half // 2).astype(F32)
    live = (z_freq >= down[:, 0:1]) & (z_freq < down[:, 1:2])
    masked = jnp.where(live, coef[...].reshape(bands * sticks, width), 0.0)
    high = masked.astype(BF)
    rest = (masked - high.astype(F32)).astype(BF)
    columns = dot_t(fz[0], high) + (dot_t(fz[0], rest) + dot_t(fz[1], high))
    send1[...] = columns.reshape(send1.shape).astype(BF)
    pl.semaphore_wait(barrier, n_fft + n_band - 2)
    exchanges[0].start()

    build_cells(half, q, w1, w1t, oxl)
    for n in range(nq + 3, len(order)):
        loads[n].wait()
    exchanges[0].wait()

    spread_sticks(recv1, oxl, cfb, lhs)
    place(lhs, w1, gbox)
    count = 4
    for first in range(0, pot.shape[0], count):
        apply_potential(first, count, gbox, pot, fya, fyb, fx, fxb, ya, yb, pk)
    pick(pk, w1t, oxl, lhs, send2)
    exchanges[1].start()

    exchanges[1].wait()

    values = recv2[...].reshape(-1, bands * sticks)
    local = (dot(fzb[0], values) + dot(fzb[1], values)).T
    kinetic = (down[:, 2:3] + z_freq * z_freq) * (2.0 / (half * half))
    h = jnp.where(live, kinetic * masked + local, 0.0)
    group = sticks // n_band
    for r in range(n_band):
        one, two = r * group, sticks + r * group
        a, b = h[one : one + group], h[two : two + group]
        tail = join([a[:, LANES:], b[:, LANES:]], 1)
        send3[r] = join([a[:, :LANES], b[:, :LANES], tail], 0).astype(BF)
    exchanges[2].start()
    kept_h[...] = h.reshape(kept_h.shape)
    out_copy = pltpu.make_async_copy(kept_h, applied, out_sem)
    out_copy.start()
    exchanges[2].wait()

    ours = recv3[...].astype(F32)
    tail = ours[:, 2 * group :]
    ours = join([
        join([ours[:, :group], tail[:, :, : width - LANES]], 2)[:, None],
        join([ours[:, group : 2 * group], tail[:, :, width - LANES :]], 2)[:, None]], 1)
    ours = ours.reshape(n_band * bands, group, width)
    both = join([ours, join([ours[:, :, half:], -ours[:, :, :half]], 2)], 0)
    total = None
    for j in range(group):
        term = dot(both[:, j, :].astype(BF), orb[j])
        total = term if total is None else total + term
    total = total.T
    per = total.shape[0] // (n_band * n_fft)
    total = total.reshape(n_band, n_fft * per, total.shape[1])
    total = join([total[r] for r in range(n_band)], 1)
    for f in range(n_fft):
        send4[f] = total[per * f : per * (f + 1)]
    exchanges[3].start()
    exchanges[3].wait()
    total = recv4[0]
    for f in range(1, n_fft):
        total = total + recv4[f]
    cols = margin.shape[2]
    for r in range(n_band):
        send5[r] = total[:, cols * r : cols * (r + 1)]
    exchanges[4].start()
    exchanges[4].wait()
    pair = n_band // 2
    for part in range(2):
        total = recv5[pair * part]
        for r in range(pair * part + 1, pair * (part + 1)):
            total = total + recv5[r]
        margin[part] = total
    out_copy.wait()


def per_device(n_band, n_fft, band_coeffs, potential, stick_column, stick_length, orbitals):
    bands, sticks, width = band_coeffs.shape
    half = width // 2
    planes, grid = potential.shape[:2]
    rows = orbitals.shape[0]
    orbitals = orbitals.transpose(1, 2, 0)
    tables = dft_tables(half, grid)
    count, group = stick_column.shape[0], orbitals.shape[0]
    per = rows // (n_band * n_fft)
    cells = half // SUB * LANES
    blocks = planes * bands * 2
    first = (n_fft, 2 * planes, bands * sticks)
    swap = (n_band, bands * group * width // LANES, LANES)
    cols = 2 * n_band * bands
    fold = (n_fft, per, n_band * cols)
    last = (n_band, per, cols)
    vm, sem = pltpu.VMEM, pltpu.SemaphoreType.DMA
    n_rows = count // LANES
    full, parts = pl.pallas_call(
        functools.partial(kernel, n_band, n_fft),
        out_shape=(
            jax.ShapeDtypeStruct(band_coeffs.shape, F32), jax.ShapeDtypeStruct((2, per, cols), F32)),
        in_specs=[pl.BlockSpec(memory_space=pl.ANY)] * 13,
        out_specs=(pl.BlockSpec(memory_space=pl.ANY), pl.BlockSpec(memory_space=pltpu.VMEM)),
        scratch_shapes=[
            vm(band_coeffs.shape, F32), vm(potential.shape, F32), vm((n_rows, LANES), I32),
            vm((1, sticks), I32), vm(orbitals.shape, BF)]
        + [vm(t.shape, BF) for t in tables]
        + [
            vm((count, cells), BF), vm((cells, count), BF), vm((SUB, count), F32),
            vm((bands, 2 * planes, count), F32), vm((SUB * blocks, count), BF),
            vm((blocks, half, LANES), BF), vm((SUB * blocks, cells), BF)]
        + [vm(first, BF)] * 4 + [vm(swap, BF)] * 2 + [vm(fold, F32)] * 2 + [vm(last, F32)] * 2
        + [vm(band_coeffs.shape, F32), sem(()), sem((n_rows + 12,)), sem((3, n_fft)), sem((3, n_fft)), sem((2, n_band)), sem((2, n_band))],
        compiler_params=pltpu.CompilerParams(
            collective_id=0, has_side_effects=True, vmem_limit_bytes=60 * 1024 * 1024),
        name="hamiltonian",
    )(band_coeffs, potential, stick_column, stick_length, orbitals, *[jnp.asarray(t) for t in tables])
    def finish(full_ref, parts_ref, applied_ref, margin_ref):
        applied_ref[...] = full_ref[...].astype(BF)
        margin_ref[...] = parts_ref[0] + parts_ref[1]

    return pl.pallas_call(
        finish,
        out_shape=(jax.ShapeDtypeStruct(band_coeffs.shape, BF), jax.ShapeDtypeStruct((per, cols), F32)),
        in_specs=[pl.BlockSpec(memory_space=pltpu.VMEM)] * 2,
        out_specs=(pl.BlockSpec(memory_space=pltpu.VMEM),) * 2,
        name="finish",
    )(full, parts)


def solution(mesh):
    placed = (
        P("band", "fft", None),
        P("fft", None, None),
        P(),
        P("fft"),
        P(None, ("band", "fft"), None),
    )
    return jax.shard_map(
        functools.partial(per_device, mesh.shape["band"], mesh.shape["fft"]),
        mesh=mesh,
        in_specs=placed,
        out_specs=(P("band", "fft", None), P(("band", "fft"), None)),
        check_vma=False,
    )
```

```python
import functools
import math

import jax
import jax.numpy as jnp
import numpy as np
from jax import lax
from jax.experimental import pallas as pl
from jax.experimental.pallas import tpu as pltpu
from jax.sharding import PartitionSpec as P

BF = jnp.bfloat16
F32 = jnp.float32
I32 = jnp.int32
MESH = pl.DeviceIdType.MESH
LANES = 128
SUB = 8


def dft_tables(half, grid):
    freq = np.arange(half) - half // 2
    angle = (freq[:, None] * np.arange(grid)[None, :] % grid) * (2.0 * math.pi / grid)
    co, si = np.cos(angle), np.sin(angle)
    cp, sp = (np.concatenate([a, np.zeros((LANES - half, grid))], 0) for a in (co, si))
    near, far = slice(0, LANES), slice(LANES, grid)

    def ahead(part):
        return (np.concatenate([cp[:, part], -sp[:, part]], 0),
                np.concatenate([sp[:, part], cp[:, part]], 0))

    def back(part):
        return (np.concatenate([cp[:, part].T, -sp[:, part].T], 1),
                np.concatenate([sp[:, part].T, cp[:, part].T], 1))

    y_near = np.concatenate(ahead(near), 1)
    r, i = ahead(far)
    o = np.zeros_like(r)
    y_far = np.concatenate([np.concatenate([r, o, i, o], 1), np.concatenate([o, r, o, i], 1)], 0)
    order = np.concatenate([np.arange(0, half, 2), np.arange(1, half, 2)])
    cx, sx = co[order], si[order]
    x_ahead = np.concatenate(
        [np.concatenate([cx.T, -sx.T], 1), np.concatenate([sx.T, cx.T], 1)], 0)
    parts = []
    for part in (slice(0, half // 2), slice(half // 2, half)):
        c, s = cx[part, : grid // 2], sx[part, : grid // 2]
        parts.append(np.concatenate([np.concatenate([c, s], 1), np.concatenate([-s, c], 1)], 0))
    x_back = np.stack(parts)
    yb_near = np.concatenate(back(near), 0)
    r, i = back(far)
    o = np.zeros_like(r)
    yb_far = np.concatenate([np.concatenate([r, o, i, o], 0), np.concatenate([o, r, o, i], 0)], 1)
    z_ahead = np.stack(
        [np.concatenate([co.T, -si.T], 1), np.concatenate([si.T, co.T], 1)], 1
    ).reshape(2 * grid, 2 * half)
    z_back = np.concatenate(
        [np.stack([co, si], -1).reshape(half, -1), np.stack([-si, co], -1).reshape(half, -1)], 0
    ) / float(grid) ** 3

    def two_part(a):
        high = a.astype(np.float32).astype(BF)
        low = (a - high.astype(np.float64)).astype(np.float32).astype(BF)
        return np.stack([high, low])

    plain = [a.astype(np.float32).astype(BF) for a in (y_near, y_far, x_ahead, x_back, yb_near, yb_far)]
    return [two_part(z_ahead)] + plain + [two_part(z_back)]


def dot(a, b):
    return jnp.dot(a, b, preferred_element_type=F32)


def dot_t(a, b):
    return lax.dot_general(a, b, (((1,), (1,)), ((), ())), preferred_element_type=F32)


def iota(shape, dim):
    return lax.broadcasted_iota(I32, shape, dim)


def join(parts, axis):
    return jnp.concatenate(parts, axis=axis)


DIGITS = {"fft": ((2, 1), (4, 1), (2, 0)), "band": ((2, 2), (4, 1))}


def partners(axis, n):
    digits = DIGITS[axis]
    assert math.prod(size for size, _ in digits) == n
    me = lax.axis_index(axis)
    mine, offsets, stride = [], [()], n
    for size, _ in digits:
        stride //= size
        mine.append((lax.rem(me // stride, size), size, stride))
        offsets = [o + (k,) for o in offsets for k in range(size)]

    def hops(offset):
        return sum(min(k, size - k) * cost for k, (size, cost) in zip(offset, digits))

    found = []
    for k, offset in sorted(enumerate(offsets), key=lambda item: -hops(item[1])):
        if k:
            found.append((k, sum(
                lax.rem(at + step, size) * stride for step, (at, size, stride) in zip(offset, mine))))
    return found


class Exchange:
    def __init__(self, axis, n, src, dst, send_sem, recv_sem):
        me = lax.axis_index(axis)
        self.copies = []
        for k, peer in partners(axis, n):
            self.copies.append(pltpu.make_async_remote_copy(
                src_ref=src.at[peer], dst_ref=dst.at[me],
                send_sem=send_sem.at[k], recv_sem=recv_sem.at[k],
                device_id={axis: peer}, device_id_type=MESH))
        self.own = pltpu.make_async_copy(src.at[me], dst.at[me], send_sem.at[0])

    def start(self):
        for copy in self.copies:
            copy.start()
        self.own.start()

    def wait(self):
        self.own.wait()
        for copy in self.copies:
            copy.wait()


def build_cells(half, q, w1, w1t, oxl):
    qq = q[...]
    xs = qq // half
    ys = qq - xs * half
    xs = lax.rem(xs, 2) * (half // 2) + xs // 2
    xh = xs // SUB
    xl = xs - xh * SUB
    cell = xh * LANES + ys
    down = cell.astype(F32).T
    cells, rows = w1t.shape[0], qq.shape[0]
    for k in range(rows):
        sl = slice(LANES * k, LANES * (k + 1))
        w1t[:, sl] = (iota((cells, LANES), 0) == cell[k : k + 1, :]).astype(F32).astype(BF)
        w1[sl, :] = (iota((LANES, cells), 1).astype(F32) == down[:, k : k + 1]).astype(F32).astype(BF)
        oxl[:, sl] = (iota((SUB, LANES), 0) == xl[k : k + 1, :]).astype(F32)


def spread_sticks(recv, oxl, cfb, lhs):
    nf, rows, lanes = recv.shape
    low = iota((rows, lanes), 1) < lanes // 2
    for k in range(nf // 2):
        a = recv[2 * k].astype(F32)
        b = recv[2 * k + 1].astype(F32)
        sl = slice(lanes * k, lanes * (k + 1))
        cfb[0, :, sl] = jnp.where(low, a, pltpu.roll(b, lanes // 2, 1))
        cfb[1, :, sl] = jnp.where(low, pltpu.roll(a, lanes // 2, 1), b)
    count = cfb.shape[2]
    for p in range(rows // 2):
        blk = [
            oxl[...] * jnp.broadcast_to(cfb[b, 2 * p + c : 2 * p + c + 1, :], (SUB, count))
            for b in range(2) for c in range(2)
        ]
        lhs[4 * SUB * p : 4 * SUB * (p + 1), :] = join(blk, 0).astype(BF)


def place(lhs, w1, gbox):
    blocks, half, _ = gbox.shape
    for t in range(half // (2 * SUB)):
        o = dot(lhs[...], w1[:, 2 * LANES * t : 2 * LANES * (t + 1)])
        o = join([o[:, :LANES].reshape(blocks, SUB, LANES), o[:, LANES:].reshape(blocks, SUB, LANES)], 1)
        gbox[:, 2 * SUB * t : 2 * SUB * (t + 1), :] = o.astype(BF)


def apply_potential(first, count, gbox, pot, fya, fyb, fx, fxb, ya, yb, pk):
    half, grid = gbox.shape[1], pot.shape[1]
    wide = 3 * LANES
    planes = range(count)
    ls = []
    for d in planes:
        base = 4 * (first + d)
        for b in range(2):
            ls.append(join([gbox[base + 2 * b], gbox[base + 2 * b + 1]], 1))
    near = dot(join(ls, 0), fya[...]).astype(BF)
    far = dot(join([join([ls[2 * d], ls[2 * d + 1]], 1) for d in planes], 0), fyb[...]).astype(BF)
    cols = []
    for d in planes:
        a0 = near[2 * half * d : 2 * half * d + half]
        a2 = near[2 * half * d + half : 2 * half * (d + 1)]
        a1 = far[half * d : half * (d + 1)]
        for a in (a0, a1, a2):
            cols.append(join([a[:, :LANES], a[:, LANES:]], 0))
    psi = dot(fx[...], join(cols, 1))
    vs = []
    for d in planes:
        v = pot[first + d]
        v0, v1 = v[:, :LANES], v[:, LANES:]
        vs += [v0, join([v1, v1], 1), v0]
    vv = join(vs, 1)
    re, im = psi[:grid] * vv, psi[grid:] * vv
    mid, quarter = grid // 2, half // 2
    even = dot(fxb[0], join([re[:mid] + re[mid:], im[:mid] + im[mid:]], 0).astype(BF))
    odd = dot(fxb[1], join([re[:mid] - re[mid:], im[:mid] - im[mid:]], 0).astype(BF))
    bb = join([even[:quarter], odd[:quarter], even[quarter:], odd[quarter:]], 0).astype(BF)
    p1, p2 = [], []
    for d in planes:
        def piece(j):
            sl = slice(wide * d + LANES * j, wide * d + LANES * (j + 1))
            return join([bb[:half, sl], bb[half:, sl]], 1)
        p1 += [piece(0), piece(2)]
        p2.append(piece(1))
    c1 = dot(join(p1, 0), ya[...])
    c2 = dot(join(p2, 0), yb[...])
    per_band = pk.shape[0] // 2
    for d in planes:
        for b in range(2):
            at = 2 * half * d + half * b
            cc = c1[at : at + half] + c2[half * d : half * (d + 1), 2 * LANES * b : 2 * LANES * (b + 1)]
            rows = [
                join([cc[SUB * h : SUB * (h + 1), LANES * c : LANES * (c + 1)] for h in range(half // SUB)], 1)
                for c in range(2)
            ]
            to = per_band * b + 2 * SUB * (first + d)
            pk[to : to + 2 * SUB, :] = join(rows, 0).astype(BF)


def pick(pk, w1t, oxl, kept, out):
    rows = pk.shape[0]
    blocks = rows // SUB
    per_band = blocks // 2
    ones = (iota((blocks, rows), 1) // SUB == iota((blocks, rows), 0)).astype(F32).astype(BF)
    low = iota((per_band, LANES), 1) < LANES // 2
    step = 2 * LANES
    for t in range(w1t.shape[1] // step):
        sl = slice(step * t, step * (t + 1))
        d = dot(pk[...], w1t[:, sl])
        kept[:, sl] = (d.reshape(blocks, SUB, step) * oxl[:, sl][None]).reshape(rows, step).astype(BF)
    s = dot(ones, kept[...])
    for h in range(out.shape[0] // 2):
        lanes = slice(LANES * h, LANES * (h + 1))
        d0, d1 = s[:per_band, lanes], s[per_band:, lanes]
        out[2 * h] = jnp.where(low, d0, pltpu.roll(d1, LANES // 2, 1)).astype(BF)
        out[2 * h + 1] = jnp.where(low, pltpu.roll(d0, LANES // 2, 1), d1).astype(BF)


def kernel(
    n_band, n_fft, coef_h, pot_h, col_h, len_h, orb_h, fz_h, fya_h, fyb_h, fx_h, fxb_h, ya_h, yb_h, fzb_h,
    applied, margin,
    coef, pot, q, length, orb, fz, fya, fyb, fx, fxb, ya, yb, fzb,
    w1, w1t, oxl, cfb, lhs, gbox, pk,
    send1, recv1, send2, recv2, send3, recv3, send4, recv4, send5, recv5,
    load_sem, fft_send, fft_recv, band_send, band_recv,
):
    barrier = pltpu.get_barrier_semaphore()
    for axis, n in (("fft", n_fft), ("band", n_band)):
        for _, peer in partners(axis, n):
            pl.semaphore_signal(barrier, inc=1, device_id={axis: peer}, device_id_type=MESH)
    loads = {}
    order = [
        (len_h, length.at[0])] + [
        (col_h.at[pl.ds(LANES * k, LANES)], q.at[k]) for k in range(q.shape[0])] + [
        (coef_h, coef), (fz_h, fz), (pot_h, pot), (fya_h, fya), (fyb_h, fyb), (fx_h, fx), (fxb_h, fxb),
        (ya_h, ya), (yb_h, yb), (orb_h, orb), (fzb_h, fzb)]
    for n, (src, dst) in enumerate(order):
        loads[n] = pltpu.make_async_copy(src, dst, load_sem.at[n])
        loads[n].start()
    nq = q.shape[0]

    exchanges = [
        Exchange("fft", n_fft, send1, recv1, fft_send.at[0], fft_recv.at[0]),
        Exchange("fft", n_fft, send2, recv2, fft_send.at[1], fft_recv.at[1]),
        Exchange("band", n_band, send3, recv3, band_send.at[0], band_recv.at[0]),
        Exchange("fft", n_fft, send4, recv4, fft_send.at[2], fft_recv.at[2]),
        Exchange("band", n_band, send5, recv5, band_send.at[1], band_recv.at[1]),
    ]

    bands, sticks, width = coef.shape
    half = width // 2
    for n in range(nq + 3):
        loads[n].wait()
    me = lax.axis_index("fft")
    row = jnp.sum(jnp.where(iota(q.shape, 0) == me // 2, q[...], 0), axis=0, keepdims=True)
    row = jnp.broadcast_to(row, (SUB, LANES))
    turned = pltpu.roll(row, sticks, 1)
    low = iota((SUB, LANES), 1) < sticks
    row = jnp.where(low == (lax.rem(me, 2) == 0), row, turned)
    x_freq = row // half
    y_freq = row - x_freq * half - half // 2
    x_freq = x_freq - half // 2
    size = join([length[...]] * bands, 1)
    size = jnp.broadcast_to(size, (SUB, LANES))
    below = size // 2
    which = iota((SUB, LANES), 0)
    rows = jnp.where(which == 0, -below, jnp.where(which == 1, size - below, x_freq * x_freq + y_freq * y_freq))
    down = rows.astype(F32).T
    z_freq = iota((bands * sticks, width), 1)
    z_freq = (jnp.where(z_freq >= half, z_freq - half, z_freq) - half // 2).astype(F32)
    live = (z_freq >= down[:, 0:1]) & (z_freq < down[:, 1:2])
    masked = jnp.where(live, coef[...].reshape(bands * sticks, width), 0.0)
    high = masked.astype(BF)
    rest = (masked - high.astype(F32)).astype(BF)
    columns = dot_t(fz[0], high) + (dot_t(fz[0], rest) + dot_t(fz[1], high))
    send1[...] = columns.reshape(send1.shape).astype(BF)
    pl.semaphore_wait(barrier, n_fft + n_band - 2)
    exchanges[0].start()

    build_cells(half, q, w1, w1t, oxl)
    for n in range(nq + 3, len(order)):
        loads[n].wait()
    exchanges[0].wait()

    spread_sticks(recv1, oxl, cfb, lhs)
    place(lhs, w1, gbox)
    count = 4
    for first in range(0, pot.shape[0], count):
        apply_potential(first, count, gbox, pot, fya, fyb, fx, fxb, ya, yb, pk)
    pick(pk, w1t, oxl, lhs, send2)
    exchanges[1].start()

    exchanges[1].wait()

    values = recv2[...].reshape(-1, bands * sticks)
    local = (dot(fzb[0], values) + dot(fzb[1], values)).T
    kinetic = (down[:, 2:3] + z_freq * z_freq) * (2.0 / (half * half))
    h = jnp.where(live, kinetic * masked + local, 0.0)
    group = sticks // n_band
    for r in range(n_band):
        one, two = r * group, sticks + r * group
        a, b = h[one : one + group], h[two : two + group]
        tail = join([a[:, LANES:], b[:, LANES:]], 1)
        send3[r] = join([a[:, :LANES], b[:, :LANES], tail], 0).astype(BF)
    exchanges[2].start()
    applied[...] = h.reshape(applied.shape)
    exchanges[2].wait()

    ours = recv3[...].astype(F32)
    tail = ours[:, 2 * group :]
    ours = join([
        join([ours[:, :group], tail[:, :, : width - LANES]], 2)[:, None],
        join([ours[:, group : 2 * group], tail[:, :, width - LANES :]], 2)[:, None]], 1)
    ours = ours.reshape(n_band * bands, group, width)
    both = join([ours, join([ours[:, :, half:], -ours[:, :, :half]], 2)], 0)
    total = None
    for j in range(group):
        term = dot(both[:, j, :].astype(BF), orb[j])
        total = term if total is None else total + term
    total = total.T
    per = total.shape[0] // (n_band * n_fft)
    total = total.reshape(n_band, n_fft * per, total.shape[1])
    total = join([total[r] for r in range(n_band)], 1)
    for f in range(n_fft):
        send4[f] = total[per * f : per * (f + 1)]
    exchanges[3].start()
    exchanges[3].wait()
    total = recv4[0]
    for f in range(1, n_fft):
        total = total + recv4[f]
    cols = margin.shape[2]
    for r in range(n_band):
        send5[r] = total[:, cols * r : cols * (r + 1)]
    exchanges[4].start()
    exchanges[4].wait()
    pair = n_band // 2
    for part in range(2):
        total = recv5[pair * part]
        for r in range(pair * part + 1, pair * (part + 1)):
            total = total + recv5[r]
        margin[part] = total


def per_device(n_band, n_fft, band_coeffs, potential, stick_column, stick_length, orbitals):
    bands, sticks, width = band_coeffs.shape
    half = width // 2
    planes, grid = potential.shape[:2]
    rows = orbitals.shape[0]
    orbitals = orbitals.transpose(1, 2, 0)
    tables = dft_tables(half, grid)
    count, group = stick_column.shape[0], orbitals.shape[0]
    per = rows // (n_band * n_fft)
    cells = half // SUB * LANES
    blocks = planes * bands * 2
    first = (n_fft, 2 * planes, bands * sticks)
    swap = (n_band, bands * group * width // LANES, LANES)
    cols = 2 * n_band * bands
    fold = (n_fft, per, n_band * cols)
    last = (n_band, per, cols)
    vm, sem = pltpu.VMEM, pltpu.SemaphoreType.DMA
    n_rows = count // LANES
    full, parts = pl.pallas_call(
        functools.partial(kernel, n_band, n_fft),
        out_shape=(
            pltpu.VMEM(band_coeffs.shape, F32), pltpu.VMEM((2, per, cols), F32)),
        in_specs=[pl.BlockSpec(memory_space=pl.ANY)] * 13,
        out_specs=(pl.BlockSpec(memory_space=pltpu.VMEM),) * 2,
        scratch_shapes=[
            vm(band_coeffs.shape, F32), vm(potential.shape, F32), vm((n_rows, LANES), I32),
            vm((1, sticks), I32), vm(orbitals.shape, BF)]
        + [vm(t.shape, BF) for t in tables]
        + [
            vm((count, cells), BF), vm((cells, count), BF), vm((SUB, count), F32),
            vm((bands, 2 * planes, count), F32), vm((SUB * blocks, count), BF),
            vm((blocks, half, LANES), BF), vm((SUB * blocks, cells), BF)]
        + [vm(first, BF)] * 4 + [vm(swap, BF)] * 2 + [vm(fold, F32)] * 2 + [vm(last, F32)] * 2
        + [sem((n_rows + 12,)), sem((3, n_fft)), sem((3, n_fft)), sem((2, n_band)), sem((2, n_band))],
        compiler_params=pltpu.CompilerParams(
            collective_id=0, has_side_effects=True, vmem_limit_bytes=54 * 1024 * 1024),
        name="hamiltonian",
    )(band_coeffs, potential, stick_column, stick_length, orbitals, *[jnp.asarray(t) for t in tables])
    def finish(full_ref, parts_ref, applied_ref, margin_ref):
        applied_ref[...] = full_ref[...].astype(BF)
        margin_ref[...] = parts_ref[0] + parts_ref[1]

    return pl.pallas_call(
        finish,
        out_shape=(jax.ShapeDtypeStruct(band_coeffs.shape, BF), jax.ShapeDtypeStruct((per, cols), F32)),
        in_specs=[pl.BlockSpec(memory_space=pltpu.VMEM)] * 2,
        out_specs=(pl.BlockSpec(memory_space=pltpu.VMEM),) * 2,
        compiler_params=pltpu.CompilerParams(vmem_limit_bytes=4 * 1024 * 1024),
        name="finish",
    )(full, parts)


def solution(mesh):
    placed = (
        P("band", "fft", None),
        P("fft", None, None),
        P(),
        P("fft"),
        P(None, ("band", "fft"), None),
    )
    return jax.shard_map(
        functools.partial(per_device, mesh.shape["band"], mesh.shape["fft"]),
        mesh=mesh,
        in_specs=placed,
        out_specs=(P("band", "fft", None), P(("band", "fft"), None)),
        check_vma=False,
    )
```

```python
import functools
import math

import jax
import jax.numpy as jnp
import numpy as np
from jax import lax
from jax.experimental import pallas as pl
from jax.experimental.pallas import tpu as pltpu
from jax.sharding import PartitionSpec as P

BF = jnp.bfloat16
F32 = jnp.float32
I32 = jnp.int32
MESH = pl.DeviceIdType.MESH
LANES = 128
SUB = 8


def dft_tables(half, grid):
    freq = np.arange(half) - half // 2
    angle = (freq[:, None] * np.arange(grid)[None, :] % grid) * (2.0 * math.pi / grid)
    co, si = np.cos(angle), np.sin(angle)
    cp, sp = (np.concatenate([a, np.zeros((LANES - half, grid))], 0) for a in (co, si))
    near, far = slice(0, LANES), slice(LANES, grid)

    def ahead(part):
        return (np.concatenate([cp[:, part], -sp[:, part]], 0),
                np.concatenate([sp[:, part], cp[:, part]], 0))

    def back(part):
        return (np.concatenate([cp[:, part].T, -sp[:, part].T], 1),
                np.concatenate([sp[:, part].T, cp[:, part].T], 1))

    y_near = np.concatenate(ahead(near), 1)
    r, i = ahead(far)
    o = np.zeros_like(r)
    y_far = np.concatenate([np.concatenate([r, o, i, o], 1), np.concatenate([o, r, o, i], 1)], 0)
    order = np.concatenate([np.arange(0, half, 2), np.arange(1, half, 2)])
    cx, sx = co[order], si[order]
    x_ahead = np.concatenate(
        [np.concatenate([cx.T, -sx.T], 1), np.concatenate([sx.T, cx.T], 1)], 0)
    parts = []
    for part in (slice(0, half // 2), slice(half // 2, half)):
        c, s = cx[part, : grid // 2], sx[part, : grid // 2]
        parts.append(np.concatenate([np.concatenate([c, s], 1), np.concatenate([-s, c], 1)], 0))
    x_back = np.stack(parts)
    yb_near = np.concatenate(back(near), 0)
    r, i = back(far)
    o = np.zeros_like(r)
    yb_far = np.concatenate([np.concatenate([r, o, i, o], 0), np.concatenate([o, r, o, i], 0)], 1)
    z_ahead = np.stack(
        [np.concatenate([co.T, -si.T], 1), np.concatenate([si.T, co.T], 1)], 1
    ).reshape(2 * grid, 2 * half)
    z_back = np.concatenate(
        [np.stack([co, si], -1).reshape(half, -1), np.stack([-si, co], -1).reshape(half, -1)], 0
    ) / float(grid) ** 3

    def two_part(a):
        high = a.astype(np.float32).astype(BF)
        low = (a - high.astype(np.float64)).astype(np.float32).astype(BF)
        return np.stack([high, low])

    plain = [a.astype(np.float32).astype(BF) for a in (y_near, y_far, x_ahead, x_back, yb_near, yb_far)]
    return [two_part(z_ahead)] + plain + [two_part(z_back)]


def dot(a, b):
    return jnp.dot(a, b, preferred_element_type=F32)


def dot_t(a, b):
    return lax.dot_general(a, b, (((1,), (1,)), ((), ())), preferred_element_type=F32)


def iota(shape, dim):
    return lax.broadcasted_iota(I32, shape, dim)


def join(parts, axis):
    return jnp.concatenate(parts, axis=axis)


DIGITS = {"fft": ((2, 1), (4, 1), (2, 0)), "band": ((2, 2), (4, 1))}


def partners(axis, n):
    return [(k, peer) for k, _, peer in ranked(axis, n)]


def ranked(axis, n):
    digits = DIGITS[axis]
    assert math.prod(size for size, _ in digits) == n
    me = lax.axis_index(axis)
    mine, offsets, stride = [], [()], n
    for size, _ in digits:
        stride //= size
        mine.append((lax.rem(me // stride, size), size, stride))
        offsets = [o + (k,) for o in offsets for k in range(size)]

    def hops(offset):
        return sum(min(k, size - k) * cost for k, (size, cost) in zip(offset, digits))

    found = []
    for k, offset in sorted(enumerate(offsets), key=lambda item: -hops(item[1])):
        if k:
            found.append((k, hops(offset), sum(
                lax.rem(at + step, size) * stride for step, (at, size, stride) in zip(offset, mine))))
    return found


class Spread:
    def __init__(self, n_band, n_fft, src, dst, sems):
        home = {axis: lax.axis_index(axis) for axis in ("band", "fft")}
        me = home["band"] * n_fft + home["fft"]
        rows = [(0, 0, home["band"])] + [(k, far, peer) for k, far, peer in ranked("band", n_band)]
        cols = [(0, 0, home["fft"])] + [(k, far, peer) for k, far, peer in ranked("fft", n_fft)]
        pairs = [(far_b + far_f, b, f) for kb, far_b, b in rows for kf, far_f, f in cols if kb or kf]
        pairs.sort(key=lambda item: -item[0])
        self.copies = [
            pltpu.make_async_remote_copy(
                src_ref=src.at[b * n_fft + f], dst_ref=dst.at[me], send_sem=sems.at[0], recv_sem=sems.at[1],
                device_id={"band": b, "fft": f}, device_id_type=MESH)
            for _, b, f in pairs]
        self.own = pltpu.make_async_copy(src.at[me], dst.at[me], sems.at[2])
        others = pl.ds(0, n_band * n_fft - 1)
        self.all = pltpu.make_async_remote_copy(
            src_ref=src.at[others], dst_ref=dst.at[others], send_sem=sems.at[0], recv_sem=sems.at[1],
            device_id=home, device_id_type=MESH)

    def start(self):
        for copy in self.copies:
            copy.start()
        self.own.start()

    def wait(self):
        self.own.wait()
        self.all.wait_send()
        self.all.wait_recv()


class Exchange:
    def __init__(self, axis, n, src, dst, send_sem, recv_sem):
        me = lax.axis_index(axis)
        self.copies = []
        for k, peer in partners(axis, n):
            self.copies.append(pltpu.make_async_remote_copy(
                src_ref=src.at[peer], dst_ref=dst.at[me],
                send_sem=send_sem.at[k], recv_sem=recv_sem.at[k],
                device_id={axis: peer}, device_id_type=MESH))
        self.own = pltpu.make_async_copy(src.at[me], dst.at[me], send_sem.at[0])

    def start(self):
        for copy in self.copies:
            copy.start()
        self.own.start()

    def wait(self):
        self.own.wait()
        for copy in self.copies:
            copy.wait()


def build_cells(half, q, w1, w1t, oxl):
    qq = q[...]
    xs = qq // half
    ys = qq - xs * half
    xs = lax.rem(xs, 2) * (half // 2) + xs // 2
    xh = xs // SUB
    xl = xs - xh * SUB
    cell = xh * LANES + ys
    down = cell.astype(F32).T
    cells, rows = w1t.shape[0], qq.shape[0]
    for k in range(rows):
        sl = slice(LANES * k, LANES * (k + 1))
        w1t[:, sl] = (iota((cells, LANES), 0) == cell[k : k + 1, :]).astype(F32).astype(BF)
        w1[sl, :] = (iota((LANES, cells), 1).astype(F32) == down[:, k : k + 1]).astype(F32).astype(BF)
        oxl[:, sl] = (iota((SUB, LANES), 0) == xl[k : k + 1, :]).astype(F32)


def spread_sticks(recv, oxl, cfb, lhs):
    nf, rows, lanes = recv.shape
    low = iota((rows, lanes), 1) < lanes // 2
    for k in range(nf // 2):
        a = recv[2 * k].astype(F32)
        b = recv[2 * k + 1].astype(F32)
        sl = slice(lanes * k, lanes * (k + 1))
        cfb[0, :, sl] = jnp.where(low, a, pltpu.roll(b, lanes // 2, 1))
        cfb[1, :, sl] = jnp.where(low, pltpu.roll(a, lanes // 2, 1), b)
    count = cfb.shape[2]
    for p in range(rows // 2):
        blk = [
            oxl[...] * jnp.broadcast_to(cfb[b, 2 * p + c : 2 * p + c + 1, :], (SUB, count))
            for b in range(2) for c in range(2)
        ]
        lhs[4 * SUB * p : 4 * SUB * (p + 1), :] = join(blk, 0).astype(BF)


def place(lhs, w1, gbox):
    blocks, half, _ = gbox.shape
    for t in range(half // (2 * SUB)):
        o = dot(lhs[...], w1[:, 2 * LANES * t : 2 * LANES * (t + 1)])
        o = join([o[:, :LANES].reshape(blocks, SUB, LANES), o[:, LANES:].reshape(blocks, SUB, LANES)], 1)
        gbox[:, 2 * SUB * t : 2 * SUB * (t + 1), :] = o.astype(BF)


def apply_potential(first, count, gbox, pot, fya, fyb, fx, fxb, ya, yb, pk):
    half, grid = gbox.shape[1], pot.shape[1]
    wide = 3 * LANES
    planes = range(count)
    ls = []
    for d in planes:
        base = 4 * (first + d)
        for b in range(2):
            ls.append(join([gbox[base + 2 * b], gbox[base + 2 * b + 1]], 1))
    near = dot(join(ls, 0), fya[...]).astype(BF)
    far = dot(join([join([ls[2 * d], ls[2 * d + 1]], 1) for d in planes], 0), fyb[...]).astype(BF)
    cols = []
    for d in planes:
        a0 = near[2 * half * d : 2 * half * d + half]
        a2 = near[2 * half * d + half : 2 * half * (d + 1)]
        a1 = far[half * d : half * (d + 1)]
        for a in (a0, a1, a2):
            cols.append(join([a[:, :LANES], a[:, LANES:]], 0))
    psi = dot(fx[...], join(cols, 1))
    vs = []
    for d in planes:
        v = pot[first + d]
        v0, v1 = v[:, :LANES], v[:, LANES:]
        vs += [v0, join([v1, v1], 1), v0]
    vv = join(vs, 1)
    re, im = psi[:grid] * vv, psi[grid:] * vv
    mid, quarter = grid // 2, half // 2
    even = dot(fxb[0], join([re[:mid] + re[mid:], im[:mid] + im[mid:]], 0).astype(BF))
    odd = dot(fxb[1], join([re[:mid] - re[mid:], im[:mid] - im[mid:]], 0).astype(BF))
    bb = join([even[:quarter], odd[:quarter], even[quarter:], odd[quarter:]], 0).astype(BF)
    p1, p2 = [], []
    for d in planes:
        def piece(j):
            sl = slice(wide * d + LANES * j, wide * d + LANES * (j + 1))
            return join([bb[:half, sl], bb[half:, sl]], 1)
        p1 += [piece(0), piece(2)]
        p2.append(piece(1))
    c1 = dot(join(p1, 0), ya[...])
    c2 = dot(join(p2, 0), yb[...])
    per_band = pk.shape[0] // 2
    for d in planes:
        for b in range(2):
            at = 2 * half * d + half * b
            cc = c1[at : at + half] + c2[half * d : half * (d + 1), 2 * LANES * b : 2 * LANES * (b + 1)]
            rows = [
                join([cc[SUB * h : SUB * (h + 1), LANES * c : LANES * (c + 1)] for h in range(half // SUB)], 1)
                for c in range(2)
            ]
            to = per_band * b + 2 * SUB * (first + d)
            pk[to : to + 2 * SUB, :] = join(rows, 0).astype(BF)


def pick(pk, w1t, oxl, kept, out):
    rows = pk.shape[0]
    blocks = rows // SUB
    per_band = blocks // 2
    ones = (iota((blocks, rows), 1) // SUB == iota((blocks, rows), 0)).astype(F32).astype(BF)
    low = iota((per_band, LANES), 1) < LANES // 2
    step = 2 * LANES
    for t in range(w1t.shape[1] // step):
        sl = slice(step * t, step * (t + 1))
        d = dot(pk[...], w1t[:, sl])
        kept[:, sl] = (d.reshape(blocks, SUB, step) * oxl[:, sl][None]).reshape(rows, step).astype(BF)
    s = dot(ones, kept[...])
    for h in range(out.shape[0] // 2):
        lanes = slice(LANES * h, LANES * (h + 1))
        d0, d1 = s[:per_band, lanes], s[per_band:, lanes]
        out[2 * h] = jnp.where(low, d0, pltpu.roll(d1, LANES // 2, 1)).astype(BF)
        out[2 * h + 1] = jnp.where(low, pltpu.roll(d0, LANES // 2, 1), d1).astype(BF)


def kernel(
    n_band, n_fft, coef_h, pot_h, col_h, len_h, orb_h, fz_h, fya_h, fyb_h, fx_h, fxb_h, ya_h, yb_h, fzb_h,
    applied, margin,
    coef, pot, q, length, orb, fz, fya, fyb, fx, fxb, ya, yb, fzb,
    w1, w1t, oxl, cfb, lhs, gbox, pk,
    send1, recv1, send2, recv2, send3, recv3, send4, recv4,
    load_sem, fft_send, fft_recv, band_send, band_recv, all_sem,
):
    barrier = pltpu.get_barrier_semaphore()
    for axis, n in (("fft", n_fft), ("band", n_band)):
        for _, peer in partners(axis, n):
            pl.semaphore_signal(barrier, inc=1, device_id={axis: peer}, device_id_type=MESH)
    loads = {}
    order = [
        (len_h, length.at[0])] + [
        (col_h.at[pl.ds(LANES * k, LANES)], q.at[k]) for k in range(q.shape[0])] + [
        (coef_h, coef), (fz_h, fz), (pot_h, pot), (fya_h, fya), (fyb_h, fyb), (fx_h, fx), (fxb_h, fxb),
        (ya_h, ya), (yb_h, yb), (orb_h, orb), (fzb_h, fzb)]
    for n, (src, dst) in enumerate(order):
        loads[n] = pltpu.make_async_copy(src, dst, load_sem.at[n])
        loads[n].start()
    nq = q.shape[0]

    exchanges = [
        Exchange("fft", n_fft, send1, recv1, fft_send.at[0], fft_recv.at[0]),
        Exchange("fft", n_fft, send2, recv2, fft_send.at[1], fft_recv.at[1]),
        Exchange("band", n_band, send3, recv3, band_send.at[0], band_recv.at[0]),
        Spread(n_band, n_fft, send4.reshape(n_band * n_fft, *send4.shape[2:]), recv4.reshape(n_band * n_fft, *send4.shape[2:]), all_sem),
    ]

    bands, sticks, width = coef.shape
    half = width // 2
    for n in range(nq + 3):
        loads[n].wait()
    me = lax.axis_index("fft")
    row = jnp.sum(jnp.where(iota(q.shape, 0) == me // 2, q[...], 0), axis=0, keepdims=True)
    row = jnp.broadcast_to(row, (SUB, LANES))
    turned = pltpu.roll(row, sticks, 1)
    low = iota((SUB, LANES), 1) < sticks
    row = jnp.where(low == (lax.rem(me, 2) == 0), row, turned)
    x_freq = row // half
    y_freq = row - x_freq * half - half // 2
    x_freq = x_freq - half // 2
    size = join([length[...]] * bands, 1)
    size = jnp.broadcast_to(size, (SUB, LANES))
    below = size // 2
    which = iota((SUB, LANES), 0)
    rows = jnp.where(which == 0, -below, jnp.where(which == 1, size - below, x_freq * x_freq + y_freq * y_freq))
    down = rows.astype(F32).T
    z_freq = iota((bands * sticks, width), 1)
    z_freq = (jnp.where(z_freq >= half, z_freq - half, z_freq) - half // 2).astype(F32)
    live = (z_freq >= down[:, 0:1]) & (z_freq < down[:, 1:2])
    masked = jnp.where(live, coef[...].reshape(bands * sticks, width), 0.0)
    high = masked.astype(BF)
    rest = (masked - high.astype(F32)).astype(BF)
    columns = dot_t(fz[0], high) + (dot_t(fz[0], rest) + dot_t(fz[1], high))
    send1[...] = columns.reshape(send1.shape).astype(BF)
    pl.semaphore_wait(barrier, n_fft + n_band - 2)
    exchanges[0].start()

    build_cells(half, q, w1, w1t, oxl)
    for n in range(nq + 3, len(order)):
        loads[n].wait()
    exchanges[0].wait()

    spread_sticks(recv1, oxl, cfb, lhs)
    place(lhs, w1, gbox)
    count = 6
    for first in range(0, pot.shape[0], count):
        apply_potential(first, count, gbox, pot, fya, fyb, fx, fxb, ya, yb, pk)
    pick(pk, w1t, oxl, lhs, send2)
    exchanges[1].start()

    exchanges[1].wait()

    values = recv2[...].reshape(-1, bands * sticks)
    local = (dot(fzb[0], values) + dot(fzb[1], values)).T
    kinetic = (down[:, 2:3] + z_freq * z_freq) * (2.0 / (half * half))
    h = jnp.where(live, kinetic * masked + local, 0.0)
    group = sticks // n_band
    for r in range(n_band):
        one, two = r * group, sticks + r * group
        a, b = h[one : one + group], h[two : two + group]
        tail = join([a[:, LANES:], b[:, LANES:]], 1)
        send3[r] = join([a[:, :LANES], b[:, :LANES], tail], 0).astype(BF)
    exchanges[2].start()
    applied[...] = h.reshape(applied.shape)
    exchanges[2].wait()

    ours = recv3[...].astype(F32)
    tail = ours[:, 2 * group :]
    ours = join([
        join([ours[:, :group], tail[:, :, : width - LANES]], 2)[:, None],
        join([ours[:, group : 2 * group], tail[:, :, width - LANES :]], 2)[:, None]], 1)
    ours = ours.reshape(n_band * bands, group, width)
    both = join([ours, join([ours[:, :, half:], -ours[:, :, :half]], 2)], 0)
    total = None
    for j in range(group):
        term = dot(both[:, j, :].astype(BF), orb[j])
        total = term if total is None else total + term
    total = total.T
    per = margin.shape[1]
    total = total.reshape(n_band * n_fft // 2, 2 * per, total.shape[1])
    for part in range(2):
        send4[:, part] = total[:, per * part : per * (part + 1)]
    exchanges[3].start()
    exchanges[3].wait()
    for part in range(2):
        margin[part] = jnp.sum(recv4[:, part], axis=0)


def per_device(n_band, n_fft, band_coeffs, potential, stick_column, stick_length, orbitals):
    bands, sticks, width = band_coeffs.shape
    half = width // 2
    planes, grid = potential.shape[:2]
    rows = orbitals.shape[0]
    orbitals = orbitals.transpose(1, 2, 0)
    tables = dft_tables(half, grid)
    count, group = stick_column.shape[0], orbitals.shape[0]
    per = rows // (n_band * n_fft)
    cells = half // SUB * LANES
    blocks = planes * bands * 2
    first = (n_fft, 2 * planes, bands * sticks)
    swap = (n_band, bands * group * width // LANES, LANES)
    cols = 2 * n_band * bands
    share = (n_band * n_fft // 2, 2, per, cols)
    vm, sem = pltpu.VMEM, pltpu.SemaphoreType.DMA
    n_rows = count // LANES
    full, parts = pl.pallas_call(
        functools.partial(kernel, n_band, n_fft),
        out_shape=(
            pltpu.VMEM(band_coeffs.shape, F32), pltpu.VMEM((2, per, cols), F32)),
        in_specs=[pl.BlockSpec(memory_space=pl.ANY)] * 13,
        out_specs=(pl.BlockSpec(memory_space=pltpu.VMEM),) * 2,
        scratch_shapes=[
            vm(band_coeffs.shape, F32), vm(potential.shape, F32), vm((n_rows, LANES), I32),
            vm((1, sticks), I32), vm(orbitals.shape, BF)]
        + [vm(t.shape, BF) for t in tables]
        + [
            vm((count, cells), BF), vm((cells, count), BF), vm((SUB, count), F32),
            vm((bands, 2 * planes, count), F32), vm((SUB * blocks, count), BF),
            vm((blocks, half, LANES), BF), vm((SUB * blocks, cells), BF)]
        + [vm(first, BF)] * 4 + [vm(swap, BF)] * 2 + [vm(share, F32)] * 2
        + [sem((n_rows + 12,)), sem((2, n_fft)), sem((2, n_fft)), sem((1, n_band)), sem((1, n_band)), sem((3,))],
        compiler_params=pltpu.CompilerParams(
            collective_id=0, has_side_effects=True, vmem_limit_bytes=54 * 1024 * 1024),
        name="hamiltonian",
    )(band_coeffs, potential, stick_column, stick_length, orbitals, *[jnp.asarray(t) for t in tables])
    def finish(full_ref, parts_ref, applied_ref, margin_ref):
        applied_ref[...] = full_ref[...].astype(BF)
        margin_ref[...] = parts_ref[0] + parts_ref[1]

    return pl.pallas_call(
        finish,
        out_shape=(jax.ShapeDtypeStruct(band_coeffs.shape, BF), jax.ShapeDtypeStruct((per, cols), F32)),
        in_specs=[pl.BlockSpec(memory_space=pltpu.VMEM)] * 2,
        out_specs=(pl.BlockSpec(memory_space=pltpu.VMEM),) * 2,
        compiler_params=pltpu.CompilerParams(vmem_limit_bytes=4 * 1024 * 1024),
        name="finish",
    )(full, parts)


def solution(mesh):
    placed = (
        P("band", "fft", None),
        P("fft", None, None),
        P(),
        P("fft"),
        P(None, ("band", "fft"), None),
    )
    return jax.shard_map(
        functools.partial(per_device, mesh.shape["band"], mesh.shape["fft"]),
        mesh=mesh,
        in_specs=placed,
        out_specs=(P("band", "fft", None), P(("band", "fft"), None)),
        check_vma=False,
    )
```

```python
import functools
import math

import jax
import jax.numpy as jnp
import numpy as np
from jax import lax
from jax.experimental import pallas as pl
from jax.experimental.pallas import tpu as pltpu
from jax.sharding import PartitionSpec as P

BF = jnp.bfloat16
F32 = jnp.float32
I32 = jnp.int32
MESH = pl.DeviceIdType.MESH
LANES = 128
SUB = 8


def dft_tables(half, grid):
    freq = np.arange(half) - half // 2
    angle = (freq[:, None] * np.arange(grid)[None, :] % grid) * (2.0 * math.pi / grid)
    co, si = np.cos(angle), np.sin(angle)
    cp, sp = (np.concatenate([a, np.zeros((LANES - half, grid))], 0) for a in (co, si))
    near, far = slice(0, LANES), slice(LANES, grid)

    def ahead(part):
        return (np.concatenate([cp[:, part], -sp[:, part]], 0),
                np.concatenate([sp[:, part], cp[:, part]], 0))

    def back(part):
        return (np.concatenate([cp[:, part].T, -sp[:, part].T], 1),
                np.concatenate([sp[:, part].T, cp[:, part].T], 1))

    y_near = np.concatenate(ahead(near), 1)
    r, i = ahead(far)
    o = np.zeros_like(r)
    y_far = np.concatenate([np.concatenate([r, o, i, o], 1), np.concatenate([o, r, o, i], 1)], 0)
    order = np.concatenate([np.arange(0, half, 2), np.arange(1, half, 2)])
    cx, sx = co[order], si[order]
    x_ahead = np.concatenate(
        [np.concatenate([cx.T, -sx.T], 1), np.concatenate([sx.T, cx.T], 1)], 0)
    parts = []
    for part in (slice(0, half // 2), slice(half // 2, half)):
        c, s = cx[part, : grid // 2], sx[part, : grid // 2]
        parts.append(np.concatenate([np.concatenate([c, s], 1), np.concatenate([-s, c], 1)], 0))
    x_back = np.stack(parts)
    yb_near = np.concatenate(back(near), 0)
    r, i = back(far)
    o = np.zeros_like(r)
    yb_far = np.concatenate([np.concatenate([r, o, i, o], 0), np.concatenate([o, r, o, i], 0)], 1)
    z_ahead = np.stack(
        [np.concatenate([co.T, -si.T], 1), np.concatenate([si.T, co.T], 1)], 1
    ).reshape(2 * grid, 2 * half)
    z_back = np.concatenate(
        [np.stack([co, si], -1).reshape(half, -1), np.stack([-si, co], -1).reshape(half, -1)], 0
    ) / float(grid) ** 3

    def two_part(a):
        high = a.astype(np.float32).astype(BF)
        low = (a - high.astype(np.float64)).astype(np.float32).astype(BF)
        return np.stack([high, low])

    plain = [a.astype(np.float32).astype(BF) for a in (y_near, y_far, x_ahead, x_back, yb_near, yb_far)]
    return [two_part(z_ahead)] + plain + [two_part(z_back)]


def dot(a, b):
    return jnp.dot(a, b, preferred_element_type=F32)


def dot_t(a, b):
    return lax.dot_general(a, b, (((1,), (1,)), ((), ())), preferred_element_type=F32)


def iota(shape, dim):
    return lax.broadcasted_iota(I32, shape, dim)


def join(parts, axis):
    return jnp.concatenate(parts, axis=axis)


DIGITS = {"fft": ((2, 1), (4, 1), (2, 0)), "band": ((2, 2), (4, 1))}


def partners(axis, n):
    return [(k, peer) for k, _, peer in ranked(axis, n)]


def ranked(axis, n):
    digits = DIGITS[axis]
    assert math.prod(size for size, _ in digits) == n
    me = lax.axis_index(axis)
    mine, offsets, stride = [], [()], n
    for size, _ in digits:
        stride //= size
        mine.append((lax.rem(me // stride, size), size, stride))
        offsets = [o + (k,) for o in offsets for k in range(size)]

    def hops(offset):
        return sum(min(k, size - k) * cost for k, (size, cost) in zip(offset, digits))

    found = []
    for k, offset in sorted(enumerate(offsets), key=lambda item: -hops(item[1])):
        if k:
            found.append((k, hops(offset), sum(
                lax.rem(at + step, size) * stride for step, (at, size, stride) in zip(offset, mine))))
    return found


class Spread:
    def __init__(self, n_band, n_fft, src, dst, sems):
        home = {axis: lax.axis_index(axis) for axis in ("band", "fft")}
        me = home["band"] * n_fft + home["fft"]
        rows = [(0, 0, home["band"])] + [(k, far, peer) for k, far, peer in ranked("band", n_band)]
        cols = [(0, 0, home["fft"])] + [(k, far, peer) for k, far, peer in ranked("fft", n_fft)]
        pairs = [(far_b + far_f, b, f) for kb, far_b, b in rows for kf, far_f, f in cols if kb or kf]
        pairs.sort(key=lambda item: -item[0])
        self.copies = [
            pltpu.make_async_remote_copy(
                src_ref=src.at[b * n_fft + f], dst_ref=dst.at[me], send_sem=sems.at[0], recv_sem=sems.at[1],
                device_id={"band": b, "fft": f}, device_id_type=MESH)
            for _, b, f in pairs]
        self.own = pltpu.make_async_copy(src.at[me], dst.at[me], sems.at[2])
        others = pl.ds(0, n_band * n_fft - 1)
        self.all = pltpu.make_async_remote_copy(
            src_ref=src.at[others], dst_ref=dst.at[others], send_sem=sems.at[0], recv_sem=sems.at[1],
            device_id=home, device_id_type=MESH)

    def start(self):
        for copy in self.copies:
            copy.start()
        self.own.start()

    def wait(self):
        self.own.wait()
        self.all.wait_send()
        self.all.wait_recv()


class Exchange:
    def __init__(self, axis, n, src, dst, send_sem, recv_sem):
        me = lax.axis_index(axis)
        self.copies = []
        for k, peer in partners(axis, n):
            self.copies.append(pltpu.make_async_remote_copy(
                src_ref=src.at[peer], dst_ref=dst.at[me],
                send_sem=send_sem.at[k], recv_sem=recv_sem.at[k],
                device_id={axis: peer}, device_id_type=MESH))
        self.own = pltpu.make_async_copy(src.at[me], dst.at[me], send_sem.at[0])

    def start(self):
        for copy in self.copies:
            copy.start()
        self.own.start()

    def wait(self):
        self.own.wait()
        for copy in self.copies:
            copy.wait()


def build_cells(half, q, w1, w1t, oxl):
    qq = q[...]
    xs = qq // half
    ys = qq - xs * half
    xs = lax.rem(xs, 2) * (half // 2) + xs // 2
    xh = xs // SUB
    xl = xs - xh * SUB
    cell = xh * LANES + ys
    down = cell.astype(F32).T
    cells, rows = w1t.shape[0], qq.shape[0]
    for k in range(rows):
        sl = slice(LANES * k, LANES * (k + 1))
        w1t[:, sl] = (iota((cells, LANES), 0) == cell[k : k + 1, :]).astype(F32).astype(BF)
        w1[sl, :] = (iota((LANES, cells), 1).astype(F32) == down[:, k : k + 1]).astype(F32).astype(BF)
        oxl[:, sl] = (iota((SUB, LANES), 0) == xl[k : k + 1, :]).astype(F32)


def spread_sticks(recv, oxl, cfb, lhs):
    nf, rows, lanes = recv.shape
    low = iota((rows, lanes), 1) < lanes // 2
    for k in range(nf // 2):
        a = recv[2 * k].astype(F32)
        b = recv[2 * k + 1].astype(F32)
        sl = slice(lanes * k, lanes * (k + 1))
        cfb[0, :, sl] = jnp.where(low, a, pltpu.roll(b, lanes // 2, 1))
        cfb[1, :, sl] = jnp.where(low, pltpu.roll(a, lanes // 2, 1), b)
    count = cfb.shape[2]
    for p in range(rows // 2):
        blk = [
            oxl[...] * jnp.broadcast_to(cfb[b, 2 * p + c : 2 * p + c + 1, :], (SUB, count))
            for b in range(2) for c in range(2)
        ]
        lhs[4 * SUB * p : 4 * SUB * (p + 1), :] = join(blk, 0).astype(BF)


def place(lhs, w1, gbox):
    blocks, half, _ = gbox.shape
    for t in range(half // (2 * SUB)):
        o = dot(lhs[...], w1[:, 2 * LANES * t : 2 * LANES * (t + 1)])
        o = join([o[:, :LANES].reshape(blocks, SUB, LANES), o[:, LANES:].reshape(blocks, SUB, LANES)], 1)
        gbox[:, 2 * SUB * t : 2 * SUB * (t + 1), :] = o.astype(BF)


def apply_potential(first, count, gbox, pot, fya, fyb, fx, fxb, ya, yb, pk):
    half, grid = gbox.shape[1], pot.shape[1]
    wide = 3 * LANES
    planes = range(count)
    ls = []
    for d in planes:
        base = 4 * (first + d)
        for b in range(2):
            ls.append(join([gbox[base + 2 * b], gbox[base + 2 * b + 1]], 1))
    near = dot(join(ls, 0), fya[...]).astype(BF)
    far = dot(join([join([ls[2 * d], ls[2 * d + 1]], 1) for d in planes], 0), fyb[...]).astype(BF)
    cols = []
    for d in planes:
        a0 = near[2 * half * d : 2 * half * d + half]
        a2 = near[2 * half * d + half : 2 * half * (d + 1)]
        a1 = far[half * d : half * (d + 1)]
        for a in (a0, a1, a2):
            cols.append(join([a[:, :LANES], a[:, LANES:]], 0))
    psi = dot(fx[...], join(cols, 1))
    vs = []
    for d in planes:
        v = pot[first + d]
        v0, v1 = v[:, :LANES], v[:, LANES:]
        vs += [v0, join([v1, v1], 1), v0]
    vv = join(vs, 1)
    re, im = psi[:grid] * vv, psi[grid:] * vv
    mid, quarter = grid // 2, half // 2
    even = dot(fxb[0], join([re[:mid] + re[mid:], im[:mid] + im[mid:]], 0).astype(BF))
    odd = dot(fxb[1], join([re[:mid] - re[mid:], im[:mid] - im[mid:]], 0).astype(BF))
    bb = join([even[:quarter], odd[:quarter], even[quarter:], odd[quarter:]], 0).astype(BF)
    p1, p2 = [], []
    for d in planes:
        def piece(j):
            sl = slice(wide * d + LANES * j, wide * d + LANES * (j + 1))
            return join([bb[:half, sl], bb[half:, sl]], 1)
        p1 += [piece(0), piece(2)]
        p2.append(piece(1))
    c1 = dot(join(p1, 0), ya[...])
    c2 = dot(join(p2, 0), yb[...])
    per_band = pk.shape[0] // 2
    for d in planes:
        for b in range(2):
            at = 2 * half * d + half * b
            cc = c1[at : at + half] + c2[half * d : half * (d + 1), 2 * LANES * b : 2 * LANES * (b + 1)]
            rows = [
                join([cc[SUB * h : SUB * (h + 1), LANES * c : LANES * (c + 1)] for h in range(half // SUB)], 1)
                for c in range(2)
            ]
            to = per_band * b + 2 * SUB * (first + d)
            pk[to : to + 2 * SUB, :] = join(rows, 0).astype(BF)


def pick(pk, w1t, oxl, kept, out):
    rows = pk.shape[0]
    blocks = rows // SUB
    per_band = blocks // 2
    ones = (iota((blocks, rows), 1) // SUB == iota((blocks, rows), 0)).astype(F32).astype(BF)
    low = iota((per_band, LANES), 1) < LANES // 2
    step = 2 * LANES
    for t in range(w1t.shape[1] // step):
        sl = slice(step * t, step * (t + 1))
        d = dot(pk[...], w1t[:, sl])
        kept[:, sl] = (d.reshape(blocks, SUB, step) * oxl[:, sl][None]).reshape(rows, step).astype(BF)
    s = dot(ones, kept[...])
    for h in range(out.shape[0] // 2):
        lanes = slice(LANES * h, LANES * (h + 1))
        d0, d1 = s[:per_band, lanes], s[per_band:, lanes]
        out[2 * h] = jnp.where(low, d0, pltpu.roll(d1, LANES // 2, 1)).astype(BF)
        out[2 * h + 1] = jnp.where(low, pltpu.roll(d0, LANES // 2, 1), d1).astype(BF)


def kernel(
    n_band, n_fft, coef_h, pot_h, col_h, len_h, orb_h, fz_h, fya_h, fyb_h, fx_h, fxb_h, ya_h, yb_h, fzb_h,
    applied, margin,
    coef, pot, q, length, orb, fz, fya, fyb, fx, fxb, ya, yb, fzb,
    w1, w1t, oxl, cfb, lhs, gbox, pk,
    send1, recv1, send2, recv2, send3, recv3, send4, recv4, sums,
    load_sem, fft_send, fft_recv, band_send, band_recv, all_sem,
):
    barrier = pltpu.get_barrier_semaphore()
    for axis, n in (("fft", n_fft), ("band", n_band)):
        for _, peer in partners(axis, n):
            pl.semaphore_signal(barrier, inc=1, device_id={axis: peer}, device_id_type=MESH)
    loads = {}
    order = [
        (len_h, length.at[0])] + [
        (col_h.at[pl.ds(LANES * k, LANES)], q.at[k]) for k in range(q.shape[0])] + [
        (coef_h, coef), (fz_h, fz), (pot_h, pot), (fya_h, fya), (fyb_h, fyb), (fx_h, fx), (fxb_h, fxb),
        (ya_h, ya), (yb_h, yb), (orb_h, orb), (fzb_h, fzb)]
    for n, (src, dst) in enumerate(order):
        loads[n] = pltpu.make_async_copy(src, dst, load_sem.at[n])
        loads[n].start()
    nq = q.shape[0]

    exchanges = [
        Exchange("fft", n_fft, send1, recv1, fft_send.at[0], fft_recv.at[0]),
        Exchange("fft", n_fft, send2, recv2, fft_send.at[1], fft_recv.at[1]),
        Exchange("band", n_band, send3, recv3, band_send.at[0], band_recv.at[0]),
        Spread(n_band, n_fft, send4, recv4, all_sem),
    ]

    bands, sticks, width = coef.shape
    half = width // 2
    for n in range(nq + 3):
        loads[n].wait()
    me = lax.axis_index("fft")
    row = jnp.sum(jnp.where(iota(q.shape, 0) == me // 2, q[...], 0), axis=0, keepdims=True)
    row = jnp.broadcast_to(row, (SUB, LANES))
    turned = pltpu.roll(row, sticks, 1)
    low = iota((SUB, LANES), 1) < sticks
    row = jnp.where(low == (lax.rem(me, 2) == 0), row, turned)
    x_freq = row // half
    y_freq = row - x_freq * half - half // 2
    x_freq = x_freq - half // 2
    size = join([length[...]] * bands, 1)
    size = jnp.broadcast_to(size, (SUB, LANES))
    below = size // 2
    which = iota((SUB, LANES), 0)
    rows = jnp.where(which == 0, -below, jnp.where(which == 1, size - below, x_freq * x_freq + y_freq * y_freq))
    down = rows.astype(F32).T
    z_freq = iota((bands * sticks, width), 1)
    z_freq = (jnp.where(z_freq >= half, z_freq - half, z_freq) - half // 2).astype(F32)
    live = (z_freq >= down[:, 0:1]) & (z_freq < down[:, 1:2])
    masked = jnp.where(live, coef[...].reshape(bands * sticks, width), 0.0)
    high = masked.astype(BF)
    rest = (masked - high.astype(F32)).astype(BF)
    columns = dot_t(fz[0], high) + (dot_t(fz[0], rest) + dot_t(fz[1], high))
    send1[...] = columns.reshape(send1.shape).astype(BF)
    pl.semaphore_wait(barrier, n_fft + n_band - 2)
    exchanges[0].start()

    build_cells(half, q, w1, w1t, oxl)
    for n in range(nq + 3, len(order)):
        loads[n].wait()
    exchanges[0].wait()

    spread_sticks(recv1, oxl, cfb, lhs)
    place(lhs, w1, gbox)
    count = 6
    for first in range(0, pot.shape[0], count):
        apply_potential(first, count, gbox, pot, fya, fyb, fx, fxb, ya, yb, pk)
    pick(pk, w1t, oxl, lhs, send2)
    exchanges[1].start()

    exchanges[1].wait()

    values = recv2[...].reshape(-1, bands * sticks)
    local = (dot(fzb[0], values) + dot(fzb[1], values)).T
    kinetic = (down[:, 2:3] + z_freq * z_freq) * (2.0 / (half * half))
    h = jnp.where(live, kinetic * masked + local, 0.0)
    group = sticks // n_band
    for r in range(n_band):
        one, two = r * group, sticks + r * group
        a, b = h[one : one + group], h[two : two + group]
        tail = join([a[:, LANES:], b[:, LANES:]], 1)
        send3[r] = join([a[:, :LANES], b[:, :LANES], tail], 0).astype(BF)
    exchanges[2].start()
    applied[...] = h.reshape(applied.shape)
    exchanges[2].wait()

    ours = recv3[...].astype(F32)
    tail = ours[:, 2 * group :]
    ours = join([
        join([ours[:, :group], tail[:, :, : width - LANES]], 2)[:, None],
        join([ours[:, group : 2 * group], tail[:, :, width - LANES :]], 2)[:, None]], 1)
    ours = ours.reshape(n_band * bands, group, width)
    both = join([ours, join([ours[:, :, half:], -ours[:, :, :half]], 2)], 0)
    total = None
    for j in range(group):
        term = dot(both[:, j, :].astype(BF), orb[j])
        total = term if total is None else total + term
    total = total.T
    per = total.shape[0] // (n_band * n_fft)
    everyone = send4.shape[0]
    sums[...] = total
    total = join([sums[pl.ds(i, everyone, stride=per), :] for i in range(per)], 1)
    send4[...] = total.reshape(send4.shape)
    exchanges[3].start()
    exchanges[3].wait()
    for part in range(2):
        margin[part] = jnp.sum(recv4[everyone // 2 * part : everyone // 2 * (part + 1)], axis=0)


def per_device(n_band, n_fft, band_coeffs, potential, stick_column, stick_length, orbitals):
    bands, sticks, width = band_coeffs.shape
    half = width // 2
    planes, grid = potential.shape[:2]
    rows = orbitals.shape[0]
    orbitals = orbitals.transpose(1, 2, 0)
    tables = dft_tables(half, grid)
    count, group = stick_column.shape[0], orbitals.shape[0]
    per = rows // (n_band * n_fft)
    cells = half // SUB * LANES
    blocks = planes * bands * 2
    first = (n_fft, 2 * planes, bands * sticks)
    swap = (n_band, bands * group * width // LANES, LANES)
    cols = 2 * n_band * bands
    share = (n_band * n_fft, 1, per * cols)
    vm, sem = pltpu.VMEM, pltpu.SemaphoreType.DMA
    n_rows = count // LANES
    full, parts = pl.pallas_call(
        functools.partial(kernel, n_band, n_fft),
        out_shape=(
            pltpu.VMEM(band_coeffs.shape, F32), pltpu.VMEM((2, 1, per * cols), F32)),
        in_specs=[pl.BlockSpec(memory_space=pl.ANY)] * 13,
        out_specs=(pl.BlockSpec(memory_space=pltpu.VMEM),) * 2,
        scratch_shapes=[
            vm(band_coeffs.shape, F32), vm(potential.shape, F32), vm((n_rows, LANES), I32),
            vm((1, sticks), I32), vm(orbitals.shape, BF)]
        + [vm(t.shape, BF) for t in tables]
        + [
            vm((count, cells), BF), vm((cells, count), BF), vm((SUB, count), F32),
            vm((bands, 2 * planes, count), F32), vm((SUB * blocks, count), BF),
            vm((blocks, half, LANES), BF), vm((SUB * blocks, cells), BF)]
        + [vm(first, BF)] * 4 + [vm(swap, BF)] * 2 + [vm(share, F32)] * 2 + [vm((rows, cols), F32)]
        + [sem((n_rows + 12,)), sem((2, n_fft)), sem((2, n_fft)), sem((1, n_band)), sem((1, n_band)), sem((3,))],
        compiler_params=pltpu.CompilerParams(
            collective_id=0, has_side_effects=True, vmem_limit_bytes=54 * 1024 * 1024),
        name="hamiltonian",
    )(band_coeffs, potential, stick_column, stick_length, orbitals, *[jnp.asarray(t) for t in tables])
    def finish(full_ref, parts_ref, applied_ref, margin_ref):
        applied_ref[...] = full_ref[...].astype(BF)
        both = parts_ref[0] + parts_ref[1]
        margin_ref[...] = join([both[:, cols * i : cols * (i + 1)] for i in range(per)], 0)

    return pl.pallas_call(
        finish,
        out_shape=(jax.ShapeDtypeStruct(band_coeffs.shape, BF), jax.ShapeDtypeStruct((per, cols), F32)),
        in_specs=[pl.BlockSpec(memory_space=pltpu.VMEM)] * 2,
        out_specs=(pl.BlockSpec(memory_space=pltpu.VMEM),) * 2,
        compiler_params=pltpu.CompilerParams(vmem_limit_bytes=4 * 1024 * 1024),
        name="finish",
    )(full, parts)


def solution(mesh):
    placed = (
        P("band", "fft", None),
        P("fft", None, None),
        P(),
        P("fft"),
        P(None, ("band", "fft"), None),
    )
    return jax.shard_map(
        functools.partial(per_device, mesh.shape["band"], mesh.shape["fft"]),
        mesh=mesh,
        in_specs=placed,
        out_specs=(P("band", "fft", None), P(("band", "fft"), None)),
        check_vma=False,
    )
```

```python
import functools
import math

import jax
import jax.numpy as jnp
import numpy as np
from jax import lax
from jax.experimental import pallas as pl
from jax.experimental.pallas import tpu as pltpu
from jax.sharding import PartitionSpec as P

BF = jnp.bfloat16
F32 = jnp.float32
I32 = jnp.int32
MESH = pl.DeviceIdType.MESH
LANES = 128
SUB = 8


def dft_tables(half, grid):
    freq = np.arange(half) - half // 2
    angle = (freq[:, None] * np.arange(grid)[None, :] % grid) * (2.0 * math.pi / grid)
    co, si = np.cos(angle), np.sin(angle)
    cp, sp = (np.concatenate([a, np.zeros((LANES - half, grid))], 0) for a in (co, si))
    near, far = slice(0, LANES), slice(LANES, grid)

    def ahead(part):
        return (np.concatenate([cp[:, part], -sp[:, part]], 0),
                np.concatenate([sp[:, part], cp[:, part]], 0))

    def back(part):
        return (np.concatenate([cp[:, part].T, -sp[:, part].T], 1),
                np.concatenate([sp[:, part].T, cp[:, part].T], 1))

    y_near = np.concatenate(ahead(near), 1)
    r, i = ahead(far)
    o = np.zeros_like(r)
    y_far = np.concatenate([np.concatenate([r, o, i, o], 1), np.concatenate([o, r, o, i], 1)], 0)
    order = np.concatenate([np.arange(0, half, 2), np.arange(1, half, 2)])
    cx, sx = co[order], si[order]
    x_ahead = np.concatenate(
        [np.concatenate([cx.T, -sx.T], 1), np.concatenate([sx.T, cx.T], 1)], 0)
    parts = []
    for part in (slice(0, half // 2), slice(half // 2, half)):
        c, s = cx[part, : grid // 2], sx[part, : grid // 2]
        parts.append(np.concatenate([np.concatenate([c, s], 1), np.concatenate([-s, c], 1)], 0))
    x_back = np.stack(parts)
    yb_near = np.concatenate(back(near), 0)
    r, i = back(far)
    o = np.zeros_like(r)
    yb_far = np.concatenate([np.concatenate([r, o, i, o], 0), np.concatenate([o, r, o, i], 0)], 1)
    z_ahead = np.stack(
        [np.concatenate([co.T, -si.T], 1), np.concatenate([si.T, co.T], 1)], 1
    ).reshape(2 * grid, 2 * half)
    z_back = np.concatenate(
        [np.stack([co, si], -1).reshape(half, -1), np.stack([-si, co], -1).reshape(half, -1)], 0
    ) / float(grid) ** 3

    def two_part(a):
        high = a.astype(np.float32).astype(BF)
        low = (a - high.astype(np.float64)).astype(np.float32).astype(BF)
        return np.stack([high, low])

    plain = [a.astype(np.float32).astype(BF) for a in (y_near, y_far, x_ahead, x_back, yb_near, yb_far)]
    return [two_part(z_ahead)] + plain + [two_part(z_back)]


def dot(a, b):
    return jnp.dot(a, b, preferred_element_type=F32)


def dot_t(a, b):
    return lax.dot_general(a, b, (((1,), (1,)), ((), ())), preferred_element_type=F32)


def iota(shape, dim):
    return lax.broadcasted_iota(I32, shape, dim)


def join(parts, axis):
    return jnp.concatenate(parts, axis=axis)


DIGITS = {"fft": ((2, 1), (4, 1), (2, 0)), "band": ((2, 2), (4, 1))}


def partners(axis, n):
    return [(k, peer) for k, _, peer in ranked(axis, n)]


def ranked(axis, n):
    digits = DIGITS[axis]
    assert math.prod(size for size, _ in digits) == n
    me = lax.axis_index(axis)
    mine, offsets, stride = [], [()], n
    for size, _ in digits:
        stride //= size
        mine.append((lax.rem(me // stride, size), size, stride))
        offsets = [o + (k,) for o in offsets for k in range(size)]

    def hops(offset):
        return sum(min(k, size - k) * cost for k, (size, cost) in zip(offset, digits))

    found = []
    for k, offset in sorted(enumerate(offsets), key=lambda item: -hops(item[1])):
        if k:
            found.append((k, hops(offset), sum(
                lax.rem(at + step, size) * stride for step, (at, size, stride) in zip(offset, mine))))
    return found


class Spread:
    def __init__(self, n_band, n_fft, src, dst, sems):
        home = {axis: lax.axis_index(axis) for axis in ("band", "fft")}
        me = home["band"] * n_fft + home["fft"]
        half_b, half_f = n_band // 2, n_fft // 2
        rows = [(0, 0, home["band"])] + ranked("band", n_band)
        cols = [(0, 0, home["fft"])] + ranked("fft", n_fft)
        pairs = [
            (far_b + far_f - 2 * (kb >= half_b and kf >= half_f), b, f)
            for kb, far_b, b in rows for kf, far_f, f in cols if kb or kf]
        pairs.sort(key=lambda item: -item[0])
        self.copies = [
            pltpu.make_async_remote_copy(
                src_ref=src.at[b * n_fft + f], dst_ref=dst.at[me], send_sem=sems.at[0], recv_sem=sems.at[1],
                device_id={"band": b, "fft": f}, device_id_type=MESH)
            for _, b, f in pairs]
        self.own = pltpu.make_async_copy(src.at[me], dst.at[me], sems.at[2])
        others = pl.ds(0, n_band * n_fft - 1)
        self.all = pltpu.make_async_remote_copy(
            src_ref=src.at[others], dst_ref=dst.at[others], send_sem=sems.at[0], recv_sem=sems.at[1],
            device_id=home, device_id_type=MESH)

    def start(self):
        for copy in self.copies:
            copy.start()
        self.own.start()

    def wait(self):
        self.own.wait()
        self.all.wait_send()
        self.all.wait_recv()


class Exchange:
    def __init__(self, axis, n, src, dst, send_sem, recv_sem):
        me = lax.axis_index(axis)
        self.copies = []
        for k, peer in partners(axis, n):
            self.copies.append(pltpu.make_async_remote_copy(
                src_ref=src.at[peer], dst_ref=dst.at[me],
                send_sem=send_sem.at[k], recv_sem=recv_sem.at[k],
                device_id={axis: peer}, device_id_type=MESH))
        self.own = pltpu.make_async_copy(src.at[me], dst.at[me], send_sem.at[0])

    def start(self):
        for copy in self.copies:
            copy.start()
        self.own.start()

    def wait(self):
        self.own.wait()
        for copy in reversed(self.copies):
            copy.wait_recv()

    def drain(self):
        for copy in self.copies:
            copy.wait_send()


def build_cells(half, q, w1, w1t, oxl):
    qq = q[...]
    xs = qq // half
    ys = qq - xs * half
    xs = lax.rem(xs, 2) * (half // 2) + xs // 2
    xh = xs // SUB
    xl = xs - xh * SUB
    cell = xh * LANES + ys
    down = cell.astype(F32).T
    cells, rows = w1t.shape[0], qq.shape[0]
    for k in range(rows):
        sl = slice(LANES * k, LANES * (k + 1))
        w1t[:, sl] = (iota((cells, LANES), 0) == cell[k : k + 1, :]).astype(F32).astype(BF)
        w1[sl, :] = (iota((LANES, cells), 1).astype(F32) == down[:, k : k + 1]).astype(F32).astype(BF)
        oxl[:, sl] = (iota((SUB, LANES), 0) == xl[k : k + 1, :]).astype(F32)


def spread_sticks(recv, oxl, cfb, lhs):
    nf, rows, lanes = recv.shape
    low = iota((rows, lanes), 1) < lanes // 2
    for k in range(nf // 2):
        a = recv[2 * k].astype(F32)
        b = recv[2 * k + 1].astype(F32)
        sl = slice(lanes * k, lanes * (k + 1))
        cfb[0, :, sl] = jnp.where(low, a, pltpu.roll(b, lanes // 2, 1))
        cfb[1, :, sl] = jnp.where(low, pltpu.roll(a, lanes // 2, 1), b)
    count = cfb.shape[2]
    for p in range(rows // 2):
        blk = [
            oxl[...] * jnp.broadcast_to(cfb[b, 2 * p + c : 2 * p + c + 1, :], (SUB, count))
            for b in range(2) for c in range(2)
        ]
        lhs[4 * SUB * p : 4 * SUB * (p + 1), :] = join(blk, 0).astype(BF)


def place(lhs, w1, gbox):
    blocks, half, _ = gbox.shape
    for t in range(half // (2 * SUB)):
        o = dot(lhs[...], w1[:, 2 * LANES * t : 2 * LANES * (t + 1)])
        o = join([o[:, :LANES].reshape(blocks, SUB, LANES), o[:, LANES:].reshape(blocks, SUB, LANES)], 1)
        gbox[:, 2 * SUB * t : 2 * SUB * (t + 1), :] = o.astype(BF)


def apply_potential(first, count, gbox, pot, fya, fyb, fx, fxb, ya, yb, pk):
    half, grid = gbox.shape[1], pot.shape[1]
    wide = 3 * LANES
    planes = range(count)
    ls = []
    for d in planes:
        base = 4 * (first + d)
        for b in range(2):
            ls.append(join([gbox[base + 2 * b], gbox[base + 2 * b + 1]], 1))
    near = dot(join(ls, 0), fya[...]).astype(BF)
    far = dot(join([join([ls[2 * d], ls[2 * d + 1]], 1) for d in planes], 0), fyb[...]).astype(BF)
    cols = []
    for d in planes:
        a0 = near[2 * half * d : 2 * half * d + half]
        a2 = near[2 * half * d + half : 2 * half * (d + 1)]
        a1 = far[half * d : half * (d + 1)]
        for a in (a0, a1, a2):
            cols.append(join([a[:, :LANES], a[:, LANES:]], 0))
    psi = dot(fx[...], join(cols, 1))
    vs = []
    for d in planes:
        v = pot[first + d]
        v0, v1 = v[:, :LANES], v[:, LANES:]
        vs += [v0, join([v1, v1], 1), v0]
    vv = join(vs, 1)
    re, im = psi[:grid] * vv, psi[grid:] * vv
    mid, quarter = grid // 2, half // 2
    even = dot(fxb[0], join([re[:mid] + re[mid:], im[:mid] + im[mid:]], 0).astype(BF))
    odd = dot(fxb[1], join([re[:mid] - re[mid:], im[:mid] - im[mid:]], 0).astype(BF))
    bb = join([even[:quarter], odd[:quarter], even[quarter:], odd[quarter:]], 0).astype(BF)
    p1, p2 = [], []
    for d in planes:
        def piece(j):
            sl = slice(wide * d + LANES * j, wide * d + LANES * (j + 1))
            return join([bb[:half, sl], bb[half:, sl]], 1)
        p1 += [piece(0), piece(2)]
        p2.append(piece(1))
    c1 = dot(join(p1, 0), ya[...])
    c2 = dot(join(p2, 0), yb[...])
    per_band = pk.shape[0] // 2
    for d in planes:
        for b in range(2):
            at = 2 * half * d + half * b
            cc = c1[at : at + half] + c2[half * d : half * (d + 1), 2 * LANES * b : 2 * LANES * (b + 1)]
            rows = [
                join([cc[SUB * h : SUB * (h + 1), LANES * c : LANES * (c + 1)] for h in range(half // SUB)], 1)
                for c in range(2)
            ]
            to = per_band * b + 2 * SUB * (first + d)
            pk[to : to + 2 * SUB, :] = join(rows, 0).astype(BF)


def pick(pk, w1t, oxl, kept, out):
    rows = pk.shape[0]
    blocks = rows // SUB
    per_band = blocks // 2
    ones = (iota((blocks, rows), 1) // SUB == iota((blocks, rows), 0)).astype(F32).astype(BF)
    low = iota((per_band, LANES), 1) < LANES // 2
    step = 2 * LANES
    for t in range(w1t.shape[1] // step):
        sl = slice(step * t, step * (t + 1))
        d = dot(pk[...], w1t[:, sl])
        kept[:, sl] = (d.reshape(blocks, SUB, step) * oxl[:, sl][None]).reshape(rows, step).astype(BF)
    s = dot(ones, kept[...])
    for h in range(out.shape[0] // 2):
        lanes = slice(LANES * h, LANES * (h + 1))
        d0, d1 = s[:per_band, lanes], s[per_band:, lanes]
        out[2 * h] = jnp.where(low, d0, pltpu.roll(d1, LANES // 2, 1)).astype(BF)
        out[2 * h + 1] = jnp.where(low, pltpu.roll(d0, LANES // 2, 1), d1).astype(BF)


def kernel(
    n_band, n_fft, coef_h, pot_h, col_h, len_h, orb_h, fz_h, fya_h, fyb_h, fx_h, fxb_h, ya_h, yb_h, fzb_h,
    applied, margin,
    coef, pot, q, length, orb, fz, fya, fyb, fx, fxb, ya, yb, fzb,
    w1, w1t, oxl, cfb, lhs, gbox, pk,
    send1, recv1, send2, recv2, send3, recv3, send4, recv4, sums,
    load_sem, fft_send, fft_recv, band_send, band_recv, all_sem,
):
    barrier = pltpu.get_barrier_semaphore()
    for axis, n in (("fft", n_fft), ("band", n_band)):
        for _, peer in partners(axis, n):
            pl.semaphore_signal(barrier, inc=1, device_id={axis: peer}, device_id_type=MESH)
    loads = {}
    order = [
        (len_h, length.at[0])] + [
        (col_h.at[pl.ds(LANES * k, LANES)], q.at[k]) for k in range(q.shape[0])] + [
        (coef_h, coef), (fz_h, fz), (pot_h, pot), (fya_h, fya), (fyb_h, fyb), (fx_h, fx), (fxb_h, fxb),
        (ya_h, ya), (yb_h, yb), (orb_h, orb), (fzb_h, fzb)]
    for n, (src, dst) in enumerate(order):
        loads[n] = pltpu.make_async_copy(src, dst, load_sem.at[n])
        loads[n].start()
    nq = q.shape[0]

    exchanges = [
        Exchange("fft", n_fft, send1, recv1, fft_send.at[0], fft_recv.at[0]),
        Exchange("fft", n_fft, send2, recv2, fft_send.at[1], fft_recv.at[1]),
        Exchange("band", n_band, send3, recv3, band_send.at[0], band_recv.at[0]),
        Spread(n_band, n_fft, send4, recv4, all_sem),
    ]

    bands, sticks, width = coef.shape
    half = width // 2
    for n in range(nq + 3):
        loads[n].wait()
    me = lax.axis_index("fft")
    row = jnp.sum(jnp.where(iota(q.shape, 0) == me // 2, q[...], 0), axis=0, keepdims=True)
    row = jnp.broadcast_to(row, (SUB, LANES))
    turned = pltpu.roll(row, sticks, 1)
    low = iota((SUB, LANES), 1) < sticks
    row = jnp.where(low == (lax.rem(me, 2) == 0), row, turned)
    x_freq = row // half
    y_freq = row - x_freq * half - half // 2
    x_freq = x_freq - half // 2
    size = join([length[...]] * bands, 1)
    size = jnp.broadcast_to(size, (SUB, LANES))
    below = size // 2
    which = iota((SUB, LANES), 0)
    rows = jnp.where(which == 0, -below, jnp.where(which == 1, size - below, x_freq * x_freq + y_freq * y_freq))
    down = rows.astype(F32).T
    z_freq = iota((bands * sticks, width), 1)
    z_freq = (jnp.where(z_freq >= half, z_freq - half, z_freq) - half // 2).astype(F32)
    live = (z_freq >= down[:, 0:1]) & (z_freq < down[:, 1:2])
    masked = jnp.where(live, coef[...].reshape(bands * sticks, width), 0.0)
    high = masked.astype(BF)
    rest = (masked - high.astype(F32)).astype(BF)
    columns = dot_t(fz[0], high) + (dot_t(fz[0], rest) + dot_t(fz[1], high))
    send1[...] = columns.reshape(send1.shape).astype(BF)
    pl.semaphore_wait(barrier, n_fft + n_band - 2)
    exchanges[0].start()

    build_cells(half, q, w1, w1t, oxl)
    for n in range(nq + 3, len(order)):
        loads[n].wait()
    exchanges[0].wait()

    spread_sticks(recv1, oxl, cfb, lhs)
    place(lhs, w1, gbox)
    count = 6
    for first in range(0, pot.shape[0], count):
        apply_potential(first, count, gbox, pot, fya, fyb, fx, fxb, ya, yb, pk)
    pick(pk, w1t, oxl, lhs, send2)
    exchanges[1].start()
    kinetic = (down[:, 2:3] + z_freq * z_freq) * (2.0 / (half * half))
    exchanges[1].wait()

    values = recv2[...].reshape(-1, bands * sticks)
    local = (dot(fzb[0], values) + dot(fzb[1], values)).T
    h = jnp.where(live, kinetic * masked + local, 0.0)
    group = sticks // n_band
    for r in range(n_band):
        one, two = r * group, sticks + r * group
        a, b = h[one : one + group], h[two : two + group]
        tail = join([a[:, LANES:], b[:, LANES:]], 1)
        send3[r] = join([a[:, :LANES], b[:, :LANES], tail], 0).astype(BF)
    exchanges[2].start()
    applied[...] = h.reshape(applied.shape)
    exchanges[2].wait()

    ours = recv3[...].astype(F32)
    tail = ours[:, 2 * group :]
    ours = join([
        join([ours[:, :group], tail[:, :, : width - LANES]], 2)[:, None],
        join([ours[:, group : 2 * group], tail[:, :, width - LANES :]], 2)[:, None]], 1)
    ours = ours.reshape(n_band * bands, group, width)
    both = join([ours, join([ours[:, :, half:], -ours[:, :, :half]], 2)], 0)
    total = None
    for j in range(group):
        term = dot(both[:, j, :].astype(BF), orb[j])
        total = term if total is None else total + term
    total = total.T
    per = total.shape[0] // (n_band * n_fft)
    everyone = send4.shape[0]
    sums[...] = total
    total = join([sums[pl.ds(i, everyone, stride=per), :] for i in range(per)], 1)
    send4[...] = total.reshape(send4.shape)
    exchanges[3].start()
    for exchange in exchanges[:3]:
        exchange.drain()
    exchanges[3].wait()
    for part in range(2):
        margin[part] = jnp.sum(recv4[everyone // 2 * part : everyone // 2 * (part + 1)], axis=0)


def per_device(n_band, n_fft, band_coeffs, potential, stick_column, stick_length, orbitals):
    bands, sticks, width = band_coeffs.shape
    half = width // 2
    planes, grid = potential.shape[:2]
    rows = orbitals.shape[0]
    orbitals = orbitals.transpose(1, 2, 0)
    tables = dft_tables(half, grid)
    count, group = stick_column.shape[0], orbitals.shape[0]
    per = rows // (n_band * n_fft)
    cells = half // SUB * LANES
    blocks = planes * bands * 2
    first = (n_fft, 2 * planes, bands * sticks)
    swap = (n_band, bands * group * width // LANES, LANES)
    cols = 2 * n_band * bands
    share = (n_band * n_fft, 1, per * cols)
    vm, sem = pltpu.VMEM, pltpu.SemaphoreType.DMA
    n_rows = count // LANES
    full, parts = pl.pallas_call(
        functools.partial(kernel, n_band, n_fft),
        out_shape=(
            pltpu.VMEM(band_coeffs.shape, F32), pltpu.VMEM((2, 1, per * cols), F32)),
        in_specs=[pl.BlockSpec(memory_space=pl.ANY)] * 13,
        out_specs=(pl.BlockSpec(memory_space=pltpu.VMEM),) * 2,
        scratch_shapes=[
            vm(band_coeffs.shape, F32), vm(potential.shape, F32), vm((n_rows, LANES), I32),
            vm((1, sticks), I32), vm(orbitals.shape, BF)]
        + [vm(t.shape, BF) for t in tables]
        + [
            vm((count, cells), BF), vm((cells, count), BF), vm((SUB, count), F32),
            vm((bands, 2 * planes, count), F32), vm((SUB * blocks, count), BF),
            vm((blocks, half, LANES), BF), vm((SUB * blocks, cells), BF)]
        + [vm(first, BF)] * 4 + [vm(swap, BF)] * 2 + [vm(share, F32)] * 2 + [vm((rows, cols), F32)]
        + [sem((n_rows + 12,)), sem((2, n_fft)), sem((2, n_fft)), sem((1, n_band)), sem((1, n_band)), sem((3,))],
        compiler_params=pltpu.CompilerParams(
            collective_id=0, has_side_effects=True,
            vmem_limit_bytes=54 * 1024 * 1024),
        name="hamiltonian",
    )(band_coeffs, potential, stick_column, stick_length, orbitals, *[jnp.asarray(t) for t in tables])
    def finish(full_ref, parts_ref, applied_ref, margin_ref):
        applied_ref[...] = full_ref[...].astype(BF)
        both = parts_ref[0] + parts_ref[1]
        margin_ref[...] = join([both[:, cols * i : cols * (i + 1)] for i in range(per)], 0)

    return pl.pallas_call(
        finish,
        out_shape=(jax.ShapeDtypeStruct(band_coeffs.shape, BF), jax.ShapeDtypeStruct((per, cols), F32)),
        in_specs=[pl.BlockSpec(memory_space=pltpu.VMEM)] * 2,
        out_specs=(pl.BlockSpec(memory_space=pltpu.VMEM),) * 2,
        compiler_params=pltpu.CompilerParams(vmem_limit_bytes=4 * 1024 * 1024),
        name="finish",
    )(full, parts)


def solution(mesh):
    placed = (
        P("band", "fft", None),
        P("fft", None, None),
        P(),
        P("fft"),
        P(None, ("band", "fft"), None),
    )
    return jax.shard_map(
        functools.partial(per_device, mesh.shape["band"], mesh.shape["fft"]),
        mesh=mesh,
        in_specs=placed,
        out_specs=(P("band", "fft", None), P(("band", "fft"), None)),
        check_vma=False,
    )
```

```python
import functools
import math

import jax
import jax.numpy as jnp
import numpy as np
from jax import lax
from jax.experimental import pallas as pl
from jax.experimental.pallas import tpu as pltpu
from jax.sharding import PartitionSpec as P

BF = jnp.bfloat16
F32 = jnp.float32
I32 = jnp.int32
MESH = pl.DeviceIdType.MESH
LANES = 128
SUB = 8


def dft_tables(half, grid):
    freq = np.arange(half) - half // 2
    angle = (freq[:, None] * np.arange(grid)[None, :] % grid) * (2.0 * math.pi / grid)
    co, si = np.cos(angle), np.sin(angle)
    cp, sp = (np.concatenate([a, np.zeros((LANES - half, grid))], 0) for a in (co, si))
    near, far = slice(0, LANES), slice(LANES, grid)

    def ahead(part):
        return (np.concatenate([cp[:, part], -sp[:, part]], 0),
                np.concatenate([sp[:, part], cp[:, part]], 0))

    def back(part):
        return (np.concatenate([cp[:, part].T, -sp[:, part].T], 1),
                np.concatenate([sp[:, part].T, cp[:, part].T], 1))

    y_near = np.concatenate(ahead(near), 1)
    r, i = ahead(far)
    o = np.zeros_like(r)
    y_far = np.concatenate([np.concatenate([r, o, i, o], 1), np.concatenate([o, r, o, i], 1)], 0)
    order = np.concatenate([np.arange(0, half, 2), np.arange(1, half, 2)])
    cx, sx = co[order], si[order]
    x_ahead = np.concatenate(
        [np.concatenate([cx.T, -sx.T], 1), np.concatenate([sx.T, cx.T], 1)], 0)
    parts = []
    for part in (slice(0, half // 2), slice(half // 2, half)):
        c, s = cx[part, : grid // 2], sx[part, : grid // 2]
        parts.append(np.concatenate([np.concatenate([c, s], 1), np.concatenate([-s, c], 1)], 0))
    x_back = np.stack(parts)
    yb_near = np.concatenate(back(near), 0)
    r, i = back(far)
    o = np.zeros_like(r)
    yb_far = np.concatenate([np.concatenate([r, o, i, o], 0), np.concatenate([o, r, o, i], 0)], 1)
    z_ahead = np.stack(
        [np.concatenate([co.T, -si.T], 1), np.concatenate([si.T, co.T], 1)], 1
    ).reshape(2 * grid, 2 * half)
    z_back = np.concatenate(
        [np.stack([co, si], -1).reshape(half, -1), np.stack([-si, co], -1).reshape(half, -1)], 0
    ) / float(grid) ** 3

    def two_part(a):
        high = a.astype(np.float32).astype(BF)
        low = (a - high.astype(np.float64)).astype(np.float32).astype(BF)
        return np.stack([high, low])

    plain = [a.astype(np.float32).astype(BF) for a in (y_near, y_far, x_ahead, x_back, yb_near, yb_far)]
    return [two_part(z_ahead)] + plain + [two_part(z_back)]


def dot(a, b):
    return jnp.dot(a, b, preferred_element_type=F32)


def dot_t(a, b):
    return lax.dot_general(a, b, (((1,), (1,)), ((), ())), preferred_element_type=F32)


def iota(shape, dim):
    return lax.broadcasted_iota(I32, shape, dim)


def join(parts, axis):
    return jnp.concatenate(parts, axis=axis)


DIGITS = {"fft": ((2, 1), (4, 1), (2, 0)), "band": ((2, 2), (4, 1))}


def partners(axis, n):
    return [(k, peer) for k, _, peer in ranked(axis, n)]


def ranked(axis, n):
    digits = DIGITS[axis]
    assert math.prod(size for size, _ in digits) == n
    me = lax.axis_index(axis)
    mine, offsets, stride = [], [()], n
    for size, _ in digits:
        stride //= size
        mine.append((lax.rem(me // stride, size), size, stride))
        offsets = [o + (k,) for o in offsets for k in range(size)]

    def hops(offset):
        return sum(min(k, size - k) * cost for k, (size, cost) in zip(offset, digits))

    found = []
    for k, offset in sorted(enumerate(offsets), key=lambda item: -hops(item[1])):
        if k:
            found.append((k, hops(offset), sum(
                lax.rem(at + step, size) * stride for step, (at, size, stride) in zip(offset, mine))))
    return found


class Spread:
    def __init__(self, n_band, n_fft, src, dst, sems):
        home = {axis: lax.axis_index(axis) for axis in ("band", "fft")}
        me = home["band"] * n_fft + home["fft"]
        half_b, half_f = n_band // 2, n_fft // 2
        rows = [(0, 0, home["band"])] + ranked("band", n_band)
        cols = [(0, 0, home["fft"])] + ranked("fft", n_fft)
        pairs = [
            (far_b + far_f - 2 * (kb >= half_b and kf >= half_f), b, f)
            for kb, far_b, b in rows for kf, far_f, f in cols if kb or kf]
        pairs.sort(key=lambda item: -item[0])
        self.copies = [
            pltpu.make_async_remote_copy(
                src_ref=src.at[b * n_fft + f], dst_ref=dst.at[me], send_sem=sems.at[0], recv_sem=sems.at[1],
                device_id={"band": b, "fft": f}, device_id_type=MESH)
            for _, b, f in pairs]
        self.own = pltpu.make_async_copy(src.at[me], dst.at[me], sems.at[2])
        others = pl.ds(0, n_band * n_fft - 1)
        self.all = pltpu.make_async_remote_copy(
            src_ref=src.at[others], dst_ref=dst.at[others], send_sem=sems.at[0], recv_sem=sems.at[1],
            device_id=home, device_id_type=MESH)

    def start(self):
        for copy in self.copies:
            copy.start()
        self.own.start()

    def wait(self):
        self.own.wait()
        self.all.wait_send()
        self.all.wait_recv()


class Exchange:
    def __init__(self, axis, n, src, dst, send_sem, recv_sem):
        me = lax.axis_index(axis)
        self.copies = []
        for k, peer in partners(axis, n):
            self.copies.append(pltpu.make_async_remote_copy(
                src_ref=src.at[peer], dst_ref=dst.at[me],
                send_sem=send_sem.at[k], recv_sem=recv_sem.at[k],
                device_id={axis: peer}, device_id_type=MESH))
        self.own = pltpu.make_async_copy(src.at[me], dst.at[me], send_sem.at[0])

    def start(self):
        for copy in self.copies:
            copy.start()
        self.own.start()

    def wait(self):
        self.own.wait()
        for copy in reversed(self.copies):
            copy.wait_recv()

    def drain(self):
        for copy in self.copies:
            copy.wait_send()


def build_cells(half, q, w1, w1t, oxl):
    qq = q[...]
    xs = qq // half
    ys = qq - xs * half
    xs = lax.rem(xs, 2) * (half // 2) + xs // 2
    xh = xs // SUB
    xl = xs - xh * SUB
    cell = xh * LANES + ys
    down = cell.astype(F32).T
    cells, rows = w1t.shape[0], qq.shape[0]
    for k in range(rows):
        sl = slice(LANES * k, LANES * (k + 1))
        w1t[:, sl] = (iota((cells, LANES), 0) == cell[k : k + 1, :]).astype(F32).astype(BF)
        w1[sl, :] = (iota((LANES, cells), 1).astype(F32) == down[:, k : k + 1]).astype(F32).astype(BF)
        oxl[:, sl] = (iota((SUB, LANES), 0) == xl[k : k + 1, :]).astype(F32)


def spread_sticks(recv, oxl, cfb, lhs):
    nf, rows, lanes = recv.shape
    low = iota((rows, lanes), 1) < lanes // 2
    for k in range(nf // 2):
        a = recv[2 * k].astype(F32)
        b = recv[2 * k + 1].astype(F32)
        sl = slice(lanes * k, lanes * (k + 1))
        cfb[0, :, sl] = jnp.where(low, a, pltpu.roll(b, lanes // 2, 1))
        cfb[1, :, sl] = jnp.where(low, pltpu.roll(a, lanes // 2, 1), b)
    count = cfb.shape[2]
    for p in range(rows // 2):
        blk = [
            oxl[...] * jnp.broadcast_to(cfb[b, 2 * p + c : 2 * p + c + 1, :], (SUB, count))
            for b in range(2) for c in range(2)
        ]
        lhs[4 * SUB * p : 4 * SUB * (p + 1), :] = join(blk, 0).astype(BF)


def place(lhs, w1, gbox):
    blocks, half, _ = gbox.shape
    for t in range(half // (2 * SUB)):
        o = dot(lhs[...], w1[:, 2 * LANES * t : 2 * LANES * (t + 1)])
        o = join([o[:, :LANES].reshape(blocks, SUB, LANES), o[:, LANES:].reshape(blocks, SUB, LANES)], 1)
        gbox[:, 2 * SUB * t : 2 * SUB * (t + 1), :] = o.astype(BF)


def apply_potential(first, count, gbox, pot, fya, fyb, fx, fxb, ya, yb, pk):
    half, grid = gbox.shape[1], pot.shape[1]
    wide = 3 * LANES
    planes = range(count)
    ls = []
    for d in planes:
        base = 4 * (first + d)
        for b in range(2):
            ls.append(join([gbox[base + 2 * b], gbox[base + 2 * b + 1]], 1))
    near = dot(join(ls, 0), fya[...]).astype(BF)
    far = dot(join([join([ls[2 * d], ls[2 * d + 1]], 1) for d in planes], 0), fyb[...]).astype(BF)
    cols = []
    for d in planes:
        a0 = near[2 * half * d : 2 * half * d + half]
        a2 = near[2 * half * d + half : 2 * half * (d + 1)]
        a1 = far[half * d : half * (d + 1)]
        for a in (a0, a1, a2):
            cols.append(join([a[:, :LANES], a[:, LANES:]], 0))
    psi = dot(fx[...], join(cols, 1))
    vs = []
    for d in planes:
        v = pot[first + d]
        v0, v1 = v[:, :LANES], v[:, LANES:]
        vs += [v0, join([v1, v1], 1), v0]
    vv = join(vs, 1)
    re, im = psi[:grid] * vv, psi[grid:] * vv
    mid, quarter = grid // 2, half // 2
    even = dot(fxb[0], join([re[:mid] + re[mid:], im[:mid] + im[mid:]], 0).astype(BF))
    odd = dot(fxb[1], join([re[:mid] - re[mid:], im[:mid] - im[mid:]], 0).astype(BF))
    bb = join([even[:quarter], odd[:quarter], even[quarter:], odd[quarter:]], 0).astype(BF)
    p1, p2 = [], []
    for d in planes:
        def piece(j):
            sl = slice(wide * d + LANES * j, wide * d + LANES * (j + 1))
            return join([bb[:half, sl], bb[half:, sl]], 1)
        p1 += [piece(0), piece(2)]
        p2.append(piece(1))
    c1 = dot(join(p1, 0), ya[...])
    c2 = dot(join(p2, 0), yb[...])
    per_band = pk.shape[0] // 2
    for d in planes:
        for b in range(2):
            at = 2 * half * d + half * b
            cc = c1[at : at + half] + c2[half * d : half * (d + 1), 2 * LANES * b : 2 * LANES * (b + 1)]
            rows = [
                join([cc[SUB * h : SUB * (h + 1), LANES * c : LANES * (c + 1)] for h in range(half // SUB)], 1)
                for c in range(2)
            ]
            to = per_band * b + 2 * SUB * (first + d)
            pk[to : to + 2 * SUB, :] = join(rows, 0).astype(BF)


def pick(pk, w1t, oxl, kept, out):
    rows = pk.shape[0]
    blocks = rows // SUB
    per_band = blocks // 2
    ones = (iota((blocks, rows), 1) // SUB == iota((blocks, rows), 0)).astype(F32).astype(BF)
    low = iota((per_band, LANES), 1) < LANES // 2
    step = 2 * LANES
    for t in range(w1t.shape[1] // step):
        sl = slice(step * t, step * (t + 1))
        d = dot(pk[...], w1t[:, sl])
        kept[:, sl] = (d.reshape(blocks, SUB, step) * oxl[:, sl][None]).reshape(rows, step).astype(BF)
    s = dot(ones, kept[...])
    for h in range(out.shape[0] // 2):
        lanes = slice(LANES * h, LANES * (h + 1))
        d0, d1 = s[:per_band, lanes], s[per_band:, lanes]
        out[2 * h] = jnp.where(low, d0, pltpu.roll(d1, LANES // 2, 1)).astype(BF)
        out[2 * h + 1] = jnp.where(low, pltpu.roll(d0, LANES // 2, 1), d1).astype(BF)


def kernel(
    n_band, n_fft, coef_h, pot_h, col_h, len_h, orb_h, fz_h, fya_h, fyb_h, fx_h, fxb_h, ya_h, yb_h, fzb_h,
    applied, margin,
    coef, pot, q, length, orb, fz, fya, fyb, fx, fxb, ya, yb, fzb,
    w1, w1t, oxl, cfb, lhs, gbox, pk,
    send1, recv1, send2, recv2, send3, recv3, send4, recv4, sums,
    load_sem, fft_send, fft_recv, band_send, band_recv, all_sem,
):
    barrier = pltpu.get_barrier_semaphore()
    for axis, n in (("fft", n_fft), ("band", n_band)):
        for _, peer in partners(axis, n):
            pl.semaphore_signal(barrier, inc=1, device_id={axis: peer}, device_id_type=MESH)
    loads = {}
    order = [
        (len_h, length.at[0])] + [
        (col_h.at[pl.ds(LANES * k, LANES)], q.at[k]) for k in range(q.shape[0])] + [
        (coef_h, coef), (fz_h, fz), (pot_h, pot), (fya_h, fya), (fyb_h, fyb), (fx_h, fx), (fxb_h, fxb),
        (ya_h, ya), (yb_h, yb), (orb_h, orb), (fzb_h, fzb)]
    for n, (src, dst) in enumerate(order):
        loads[n] = pltpu.make_async_copy(src, dst, load_sem.at[n])
        loads[n].start()
    nq = q.shape[0]

    exchanges = [
        Exchange("fft", n_fft, send1, recv1, fft_send.at[0], fft_recv.at[0]),
        Exchange("fft", n_fft, send2, recv2, fft_send.at[1], fft_recv.at[1]),
        Exchange("band", n_band, send3, recv3, band_send.at[0], band_recv.at[0]),
        Spread(n_band, n_fft, send4, recv4, all_sem),
    ]

    bands, sticks, width = coef.shape
    half = width // 2
    for n in range(nq + 3):
        loads[n].wait()
    me = lax.axis_index("fft")
    row = jnp.sum(jnp.where(iota(q.shape, 0) == me // 2, q[...], 0), axis=0, keepdims=True)
    row = jnp.broadcast_to(row, (SUB, LANES))
    turned = pltpu.roll(row, sticks, 1)
    low = iota((SUB, LANES), 1) < sticks
    row = jnp.where(low == (lax.rem(me, 2) == 0), row, turned)
    x_freq = row // half
    y_freq = row - x_freq * half - half // 2
    x_freq = x_freq - half // 2
    size = join([length[...]] * bands, 1)
    size = jnp.broadcast_to(size, (SUB, LANES))
    below = size // 2
    which = iota((SUB, LANES), 0)
    rows = jnp.where(which == 0, -below, jnp.where(which == 1, size - below, x_freq * x_freq + y_freq * y_freq))
    down = rows.astype(F32).T
    z_freq = iota((bands * sticks, width), 1)
    z_freq = (jnp.where(z_freq >= half, z_freq - half, z_freq) - half // 2).astype(F32)
    live = (z_freq >= down[:, 0:1]) & (z_freq < down[:, 1:2])
    masked = jnp.where(live, coef[...].reshape(bands * sticks, width), 0.0)
    high = masked.astype(BF)
    rest = (masked - high.astype(F32)).astype(BF)
    columns = dot_t(fz[0], high) + (dot_t(fz[0], rest) + dot_t(fz[1], high))
    send1[...] = columns.reshape(send1.shape).astype(BF)
    pl.semaphore_wait(barrier, n_fft + n_band - 2)
    exchanges[0].start()

    build_cells(half, q, w1, w1t, oxl)
    for n in range(nq + 3, len(order)):
        loads[n].wait()
    exchanges[0].wait()

    spread_sticks(recv1, oxl, cfb, lhs)
    place(lhs, w1, gbox)
    count = 6
    for first in range(0, pot.shape[0], count):
        apply_potential(first, count, gbox, pot, fya, fyb, fx, fxb, ya, yb, pk)
    pick(pk, w1t, oxl, lhs, send2)
    exchanges[1].start()
    kinetic = (down[:, 2:3] + z_freq * z_freq) * (2.0 / (half * half))
    exchanges[1].wait()

    values = recv2[...].reshape(-1, bands * sticks)
    local = (dot(fzb[0], values) + dot(fzb[1], values)).T
    h = jnp.where(live, kinetic * masked + local, 0.0)
    group = sticks // n_band
    for r in range(n_band):
        one, two = r * group, sticks + r * group
        a, b = h[one : one + group], h[two : two + group]
        tail = join([a[:, LANES:], b[:, LANES:]], 1)
        send3[r] = join([a[:, :LANES], b[:, :LANES], tail], 0).astype(BF)
    exchanges[2].start()
    applied[...] = h.reshape(applied.shape)
    exchanges[2].wait()

    ours = recv3[...].astype(F32)
    tail = ours[:, 2 * group :]
    ours = join([
        join([ours[:, :group], tail[:, :, : width - LANES]], 2)[:, None],
        join([ours[:, group : 2 * group], tail[:, :, width - LANES :]], 2)[:, None]], 1)
    ours = ours.reshape(n_band * bands, group, width)
    both = join([ours, join([ours[:, :, half:], -ours[:, :, :half]], 2)], 0)
    stacked = join([both[:, j, :] for j in range(group)], 1).astype(BF)
    total = dot(stacked, orb[...].reshape(group * width, orb.shape[2]))
    total = total.T
    per = total.shape[0] // (n_band * n_fft)
    everyone = send4.shape[0]
    sums[...] = total
    total = join([sums[pl.ds(i, everyone, stride=per), :] for i in range(per)], 1)
    send4[...] = total.reshape(send4.shape)
    exchanges[3].start()
    for exchange in exchanges[:3]:
        exchange.drain()
    exchanges[3].wait()
    for part in range(2):
        margin[part] = jnp.sum(recv4[everyone // 2 * part : everyone // 2 * (part + 1)], axis=0)


def per_device(n_band, n_fft, band_coeffs, potential, stick_column, stick_length, orbitals):
    bands, sticks, width = band_coeffs.shape
    half = width // 2
    planes, grid = potential.shape[:2]
    rows = orbitals.shape[0]
    orbitals = orbitals.transpose(1, 2, 0)
    tables = dft_tables(half, grid)
    count, group = stick_column.shape[0], orbitals.shape[0]
    per = rows // (n_band * n_fft)
    cells = half // SUB * LANES
    blocks = planes * bands * 2
    first = (n_fft, 2 * planes, bands * sticks)
    swap = (n_band, bands * group * width // LANES, LANES)
    cols = 2 * n_band * bands
    share = (n_band * n_fft, 1, per * cols)
    vm, sem = pltpu.VMEM, pltpu.SemaphoreType.DMA
    n_rows = count // LANES
    full, parts = pl.pallas_call(
        functools.partial(kernel, n_band, n_fft),
        out_shape=(
            pltpu.VMEM(band_coeffs.shape, F32), pltpu.VMEM((2, 1, per * cols), F32)),
        in_specs=[pl.BlockSpec(memory_space=pl.ANY)] * 13,
        out_specs=(pl.BlockSpec(memory_space=pltpu.VMEM),) * 2,
        scratch_shapes=[
            vm(band_coeffs.shape, F32), vm(potential.shape, F32), vm((n_rows, LANES), I32),
            vm((1, sticks), I32), vm(orbitals.shape, BF)]
        + [vm(t.shape, BF) for t in tables]
        + [
            vm((count, cells), BF), vm((cells, count), BF), vm((SUB, count), F32),
            vm((bands, 2 * planes, count), F32), vm((SUB * blocks, count), BF),
            vm((blocks, half, LANES), BF), vm((SUB * blocks, cells), BF)]
        + [vm(first, BF)] * 4 + [vm(swap, BF)] * 2 + [vm(share, F32)] * 2 + [vm((rows, cols), F32)]
        + [sem((n_rows + 12,)), sem((2, n_fft)), sem((2, n_fft)), sem((1, n_band)), sem((1, n_band)), sem((3,))],
        compiler_params=pltpu.CompilerParams(
            collective_id=0, has_side_effects=True,
            vmem_limit_bytes=54 * 1024 * 1024),
        name="hamiltonian",
    )(band_coeffs, potential, stick_column, stick_length, orbitals, *[jnp.asarray(t) for t in tables])
    def finish(full_ref, parts_ref, applied_ref, margin_ref):
        applied_ref[...] = full_ref[...].astype(BF)
        both = parts_ref[0] + parts_ref[1]
        margin_ref[...] = join([both[:, cols * i : cols * (i + 1)] for i in range(per)], 0)

    return pl.pallas_call(
        finish,
        out_shape=(jax.ShapeDtypeStruct(band_coeffs.shape, BF), jax.ShapeDtypeStruct((per, cols), F32)),
        in_specs=[pl.BlockSpec(memory_space=pltpu.VMEM)] * 2,
        out_specs=(pl.BlockSpec(memory_space=pltpu.VMEM),) * 2,
        compiler_params=pltpu.CompilerParams(vmem_limit_bytes=4 * 1024 * 1024),
        name="finish",
    )(full, parts)


def solution(mesh):
    placed = (
        P("band", "fft", None),
        P("fft", None, None),
        P(),
        P("fft"),
        P(None, ("band", "fft"), None),
    )
    return jax.shard_map(
        functools.partial(per_device, mesh.shape["band"], mesh.shape["fft"]),
        mesh=mesh,
        in_specs=placed,
        out_specs=(P("band", "fft", None), P(("band", "fft"), None)),
        check_vma=False,
    )
```
